32 devices in a mesh: seq: 8 (over z, y), tensor: 4 (over x, core).
Axes of the slice: x: 2, y: 2, z: 4, core: 2. Of those that a mesh axis runs over, the one named last changes fastest.
Arguments:
- hidden_in: bfloat16 [1024, 2048], P('seq'), may hold values from -6 to 6
- norm_gain: float32 [2048], replicated, may hold values from 0.1 to 1.9
- query_weight: bfloat16 [2048, 2048], P(None, 'tensor'), may hold values from -0.125 to 0.125
- key_weight: bfloat16 [2048, 1024], P(None, 'tensor'), may hold values from -0.375 to 0.375
- value_weight: bfloat16 [2048, 1024], P(None, 'tensor'), may hold values from -0.125 to 0.125
- out_weight: bfloat16 [2048, 2048], P('tensor'), may hold values from -0.125 to 0.125
- key_cache: bfloat16 [512, 128, 1024], P('seq', None, 'tensor'), may hold values from -102 to 102
- value_cache: bfloat16 [512, 128, 1024], P('seq', None, 'tensor'), may hold values from -6 to 6
- cached_lengths: int32 [2], replicated, may hold values from 16385 to 32768, as said below
- group_ids: int32 [2], replicated, may hold values from 0 to 1
- prompt_pages: int32 [2, 128], replicated, may hold values from 0 to 511, as said below
- own_pages: int32 [2, 128], replicated, may hold values from 0 to 511, as said below
Outputs:
- attention_out: bfloat16 [1024, 2048], P('seq', 'tensor')
The draws below stay inside these ranges and needn't reach their ends.
Inputs may be any that keep to these rules, and one draw needn't show every extreme that they name: `cached_lengths`: each request's cache holds the 16384 tokens of its group's prompt followed by its own tokens; some request holds the most in every draw. Slot s is page s % 64 of seq index s // 64; no slot is named twice in prompt_pages and own_pages together. `own_pages`: page p of request r holds its own cached tokens from p * 128 on; entries past a request's length name slots whose contents are not read.
All inputs are finite; a program needn't handle non-finite values.
Results may differ from the reference program's by a relative error of at most 0.0055.
The reference program's roundings to bfloat16 on the way count: a program that leaves them out, or rounds other values in their place, can miss the bound.
Values may be sent and summed in bfloat16 or wider, within the bound.
A program may use at most 64 MiB of HBM per device.

```python
import math
import jax
import jax.numpy as jnp
from jax import lax

D = 2048
Q_HEADS = 16
KV_HEADS = 8
HEAD_DIM = 128
PAGE_ROWS = 128
ADDED_TOKENS = 512
REQUESTS = 2
GROUPS = 2
PROMPT_PAGES = 128
OWN_PAGES_MAX = 128
TOKENS = 1024
TOK_DEV = 128
PAGES_DEV = 64
CACHE_SLOTS = 512
N_SEQ = 8


def page_order(key):
    return jax.random.permutation(jax.random.fold_in(key, 11), CACHE_SLOTS).astype(jnp.int32)


def draw_prompt_pages(key, part):
    slot_order = page_order(key)
    return slot_order[:GROUPS * PROMPT_PAGES].reshape(GROUPS, PROMPT_PAGES)


def draw_own_pages(key, part):
    slot_order = page_order(key)
    first_own = GROUPS * PROMPT_PAGES
    return slot_order[first_own:first_own + REQUESTS * OWN_PAGES_MAX].reshape(REQUESTS, OWN_PAGES_MAX)


def draw_cached_lengths(key, part):
    own_tokens = jax.random.randint(jax.random.fold_in(key, 21), (REQUESTS,), 1, OWN_PAGES_MAX * PAGE_ROWS + 1, dtype=jnp.int32)
    longest = jax.random.randint(jax.random.fold_in(key, 22), (), 0, REQUESTS, dtype=jnp.int32)
    own_tokens = jnp.where(jnp.arange(REQUESTS, dtype=jnp.int32) == longest, OWN_PAGES_MAX * PAGE_ROWS, own_tokens)
    return (PROMPT_PAGES * PAGE_ROWS + own_tokens).astype(jnp.int32)


def draw_key_cache(key, part):
    shape = (CACHE_SLOTS, PAGE_ROWS, KV_HEADS * HEAD_DIM)
    cached = jnp.clip(jax.random.normal(jax.random.fold_in(key, 35), shape, jnp.float32) * 3.0, -12.0, 12.0)
    return cached.astype(jnp.bfloat16)


def block_scale(key, extent, split, low, top_value):
    gain, own = 1.0, jax.random.fold_in(key, 6)
    for position, parts in split:
        steps = jnp.exp(jax.random.uniform(jax.random.fold_in(own, position), (parts,), jnp.float32, low / len(split), top_value / len(split)))
        gain = gain * jnp.repeat(steps, extent[position] // parts).reshape([-1 if axis == position else 1 for axis in range(len(extent))])
    return gain


def centred(stream_key, dims, deviation, limit, cuts=(), kind=jnp.bfloat16):
    drawn = jax.random.normal(stream_key, dims, jnp.float32) * deviation
    if len(cuts) > 0:
        drawn = block_scale(stream_key, dims, cuts, -0.22, 0.18) * drawn
    return jnp.clip(drawn, min=-limit, max=limit).astype(kind)


def setup_inputs(seed: int = 0) -> dict:
    keys = jax.random.split(jax.random.key(seed), 13)
    hidden_in = centred(keys[0], (TOKENS, D), 1.0, 6.0, ((0, 8),))
    norm_gain = jnp.clip(1.0 + 0.18 * jax.random.normal(keys[1], (D,), jnp.float32), 0.1, 1.9)
    query_weight = centred(keys[2], (D, Q_HEADS * HEAD_DIM), D ** -0.5, 0.125, ((1, 4),))
    key_weight = centred(keys[3], (D, KV_HEADS * HEAD_DIM), (D // 9) ** -0.5, 0.375, ((1, 4),))
    value_weight = centred(keys[4], (D, KV_HEADS * HEAD_DIM), D ** -0.5, 0.125, ((1, 4),))
    out_weight = centred(keys[5], (Q_HEADS * HEAD_DIM, D), (Q_HEADS * HEAD_DIM) ** -0.5, 0.125, ((0, 4),))
    key_cache = draw_key_cache(jax.random.fold_in(keys[12], 71), 0)
    value_cache = centred(keys[7], (CACHE_SLOTS, PAGE_ROWS, KV_HEADS * HEAD_DIM), 1.0, 6.0, ((0, 8), (2, 4)))
    cached_lengths = draw_cached_lengths(jax.random.fold_in(keys[12], 71), 0)
    group_ids = jax.random.randint(keys[9], (REQUESTS,), 0, GROUPS).astype(jnp.int32)
    prompt_pages = draw_prompt_pages(jax.random.fold_in(keys[12], 71), 0)
    own_pages = draw_own_pages(jax.random.fold_in(keys[12], 71), 0)
    return {"hidden_in": hidden_in, "norm_gain": norm_gain, "query_weight": query_weight, "key_weight": key_weight, "value_weight": value_weight, "out_weight": out_weight, "key_cache": key_cache, "value_cache": value_cache, "cached_lengths": cached_lengths, "group_ids": group_ids, "prompt_pages": prompt_pages, "own_pages": own_pages}


def block_terms(query_grid, key_grid, value_grid, live_mask, score_scale):
    scores = jnp.einsum('qkgd,pkd->qkgp', query_grid, key_grid) * score_scale
    live_grid = live_mask[:, None, None, :]
    block_max = lax.optimization_barrier(jnp.max(jnp.where(live_grid, scores, -1e+30), axis=-1))
    weights = jnp.exp(jnp.where(live_grid, scores - block_max[..., None], -1e+30)).astype(jnp.bfloat16)
    weights_wide = lax.optimization_barrier(weights).astype(jnp.float32)
    block_sum = lax.optimization_barrier(jnp.sum(weights_wide, axis=-1))
    block_out = jnp.einsum('qkgp,pkd->qkgd', weights_wide, value_grid)
    return (block_max, block_out, block_sum)

def combine_terms(running, terms):
    run_max, run_num, run_den = running
    part_max, part_num, part_den = terms
    new_max = jnp.maximum(run_max, part_max)
    keep_scale = jnp.exp(run_max - new_max)
    add_scale = jnp.exp(part_max - new_max)
    return (new_max, run_num * keep_scale[..., None] + part_num * add_scale[..., None], run_den * keep_scale + part_den * add_scale)

def reference(hidden_in, norm_gain, query_weight, key_weight, value_weight, out_weight, key_cache, value_cache, cached_lengths, group_ids, prompt_pages, own_pages):
    floats = hidden_in.astype(jnp.float32)
    normed = (floats * lax.rsqrt(lax.optimization_barrier(jnp.mean(floats * floats, axis=-1, keepdims=True)) + 1e-05) * norm_gain).astype(jnp.bfloat16)
    queries = jnp.dot(normed, query_weight, preferred_element_type=jnp.float32).astype(jnp.bfloat16)
    keys_new = jnp.dot(normed, key_weight, preferred_element_type=jnp.float32).astype(jnp.bfloat16)
    values_new = jnp.dot(normed, value_weight, preferred_element_type=jnp.float32).astype(jnp.bfloat16)
    per_kv = Q_HEADS // KV_HEADS
    score_scale = 1.0 / math.sqrt(HEAD_DIM)
    new_blocks = ADDED_TOKENS // PAGE_ROWS
    key_pos = jnp.arange(PAGE_ROWS, dtype=jnp.int32)
    query_pos = jnp.arange(ADDED_TOKENS, dtype=jnp.int32)
    seq_ids = jnp.arange(N_SEQ, dtype=jnp.int32)

    def one_request(request):
        row_start = request * ADDED_TOKENS
        query_grid = lax.dynamic_slice_in_dim(queries, row_start, ADDED_TOKENS, 0).astype(jnp.float32)
        query_grid = query_grid.reshape(ADDED_TOKENS, KV_HEADS, per_kv, HEAD_DIM)
        group_id = lax.dynamic_index_in_dim(group_ids, request, 0, keepdims=False)
        prompt_row = lax.dynamic_index_in_dim(prompt_pages, group_id, 0, keepdims=False)
        own_row = lax.dynamic_index_in_dim(own_pages, request, 0, keepdims=False)
        own_len = lax.dynamic_index_in_dim(cached_lengths, request, 0, keepdims=False) - PROMPT_PAGES * PAGE_ROWS
        slot_ids = jnp.concatenate([prompt_row, own_row]).astype(jnp.int32)
        block_pos = jnp.arange(PROMPT_PAGES + OWN_PAGES_MAX, dtype=jnp.int32)
        live_counts = jnp.where(block_pos < PROMPT_PAGES, PAGE_ROWS, jnp.clip(own_len - (block_pos - PROMPT_PAGES) * PAGE_ROWS, 0, PAGE_ROWS)).astype(jnp.int32)
        initial = (jnp.full((N_SEQ, ADDED_TOKENS, KV_HEADS, per_kv), -1e+30, jnp.float32), jnp.zeros((N_SEQ, ADDED_TOKENS, KV_HEADS, per_kv, HEAD_DIM), jnp.float32), jnp.zeros((N_SEQ, ADDED_TOKENS, KV_HEADS, per_kv), jnp.float32))

        def cache_step(running, entry_data):
            slot_id, live_count = entry_data
            owner = (slot_id // PAGES_DEV).astype(jnp.int32)
            page_keys = lax.dynamic_index_in_dim(key_cache, slot_id, 0, keepdims=False).astype(jnp.float32)
            page_values = lax.dynamic_index_in_dim(value_cache, slot_id, 0, keepdims=False).astype(jnp.float32)
            live_mask = jnp.broadcast_to((key_pos < live_count)[None, :], (ADDED_TOKENS, PAGE_ROWS))
            terms = block_terms(query_grid, page_keys.reshape(PAGE_ROWS, KV_HEADS, HEAD_DIM), page_values.reshape(PAGE_ROWS, KV_HEADS, HEAD_DIM), live_mask, score_scale)
            current = tuple((lax.dynamic_index_in_dim(member, owner, 0, keepdims=False) for member in running))
            merged = combine_terms(current, terms)
            return (tuple((lax.dynamic_update_index_in_dim(member, updated, owner, 0) for member, updated in zip(running, merged))), None)
        running, _ = lax.scan(cache_step, initial, (slot_ids, live_counts))
        block_keys = lax.dynamic_slice_in_dim(keys_new, row_start, ADDED_TOKENS, 0).astype(jnp.float32)
        block_values = lax.dynamic_slice_in_dim(values_new, row_start, ADDED_TOKENS, 0).astype(jnp.float32)
        block_keys = block_keys.reshape(new_blocks, PAGE_ROWS, KV_HEADS, HEAD_DIM)
        block_values = block_values.reshape(new_blocks, PAGE_ROWS, KV_HEADS, HEAD_DIM)
        fresh = (jnp.full((ADDED_TOKENS, KV_HEADS, per_kv), -1e+30, jnp.float32), jnp.zeros((ADDED_TOKENS, KV_HEADS, per_kv, HEAD_DIM), jnp.float32), jnp.zeros((ADDED_TOKENS, KV_HEADS, per_kv), jnp.float32))
        for block_index in range(new_blocks):
            live_mask = (block_index * PAGE_ROWS + key_pos)[None, :] <= query_pos[:, None]
            terms = block_terms(query_grid, block_keys[block_index], block_values[block_index], live_mask, score_scale)
            fresh = combine_terms(fresh, terms)
        home = ((row_start + query_pos) // TOK_DEV).astype(jnp.int32)
        match = (home[None, :] == seq_ids[:, None])[:, :, None, None]
        placed = (jnp.where(match, fresh[0][None], -1e+30), jnp.where(match[..., None], fresh[1][None], 0.0), jnp.where(match, fresh[2][None], 0.0))
        run_max, run_num, run_den = combine_terms(running, placed)
        den_safe = jnp.maximum(run_den, 1.0)
        partial_value = (run_num / den_safe[..., None]).astype(jnp.bfloat16)
        partial_wide = lax.optimization_barrier(partial_value).astype(jnp.float32)
        log_scale = run_max + jnp.log(den_safe)
        peak = lax.optimization_barrier(jnp.max(log_scale, axis=0))
        scale_weights = jnp.exp(log_scale - peak[None])
        result = lax.optimization_barrier(jnp.sum(scale_weights[..., None] * partial_wide, axis=0)) / lax.optimization_barrier(jnp.sum(scale_weights, axis=0))[..., None]
        return result.reshape(ADDED_TOKENS, Q_HEADS * HEAD_DIM)
    attention = lax.map(one_request, jnp.arange(REQUESTS, dtype=jnp.int32))
    attention = attention.reshape(TOKENS, Q_HEADS * HEAD_DIM).astype(jnp.bfloat16)
    return jnp.dot(attention, out_weight, preferred_element_type=jnp.float32).astype(jnp.bfloat16)
```

```python
import functools
import math

import jax
import jax.numpy as jnp
from jax import lax
from jax.experimental import pallas as pl
from jax.experimental.pallas import tpu as pltpu
from jax.sharding import PartitionSpec as P

HEAD_DIM = 128
PAGE_ROWS = 128
ADDED_TOKENS = 512
GROUPS = 2
PROMPT_PAGES = 128
STEP_PAGES = 4
ROW_CHUNK = 256
SCORE_SCALE = 1.0 / math.sqrt(HEAD_DIM)
EXP2_SCALE = SCORE_SCALE * math.log2(math.e)
EMPTY = -1e30


def dot_nt(left, right):
    return lax.dot_general(
        left, right, (((1,), (1,)), ((), ())), preferred_element_type=jnp.float32
    )


def attend_kernel(
    per_kv,
    tok_rows,
    entries,
    counts,
    meta,
    q_ref,
    kn_ref,
    vn_ref,
    kc_ref,
    vc_ref,
    o_ref,
    ls_ref,
    m_ref,
    acc_ref,
):
    request = pl.program_id(0)
    heads = o_ref.shape[0]
    kv_count = heads // per_kv
    m_ref[...] = jnp.full_like(m_ref, EMPTY)
    acc_ref[...] = jnp.zeros_like(acc_ref)

    def cols(index):
        return slice(index * HEAD_DIM, (index + 1) * HEAD_DIM)

    @pl.when(meta[0] == request)
    def _():
        start = pl.multiple_of(meta[1], tok_rows)
        row = lax.broadcasted_iota(jnp.int32, (tok_rows, ADDED_TOKENS), 0)
        col = lax.broadcasted_iota(jnp.int32, (tok_rows, ADDED_TOKENS), 1)
        live = col <= row + start
        ones = jnp.ones((ADDED_TOKENS, HEAD_DIM), jnp.bfloat16)
        for head in range(heads):
            kv = head // per_kv
            scores = dot_nt(q_ref[pl.ds(start, tok_rows), cols(head)], kn_ref[:, cols(kv)])
            scores = jnp.where(live, scores, EMPTY)
            top = jnp.max(scores, axis=1, keepdims=True)
            weights = jnp.exp2((scores - top) * EXP2_SCALE).astype(jnp.bfloat16)
            values = jnp.concatenate([vn_ref[:, cols(kv)], ones], axis=1)
            m_ref[head, pl.ds(start, tok_rows), :] = jnp.broadcast_to(top, (tok_rows, HEAD_DIM))
            acc_ref[head, pl.ds(start, tok_rows), :] = jnp.dot(
                weights, values, preferred_element_type=jnp.float32
            )

    def step(index, carry):
        picked = [entries[request, index * STEP_PAGES + j] for j in range(STEP_PAGES)]
        lane = lax.broadcasted_iota(jnp.int32, (1, PAGE_ROWS), 1)
        bias = jnp.concatenate(
            [jnp.where(lane < (item & 255), 0.0, EMPTY) for item in picked], axis=1
        )
        pages = [item >> 8 for item in picked]
        ones = jnp.ones((STEP_PAGES * PAGE_ROWS, HEAD_DIM), jnp.bfloat16)
        for kv in range(kv_count):
            keys = jnp.concatenate([kc_ref[page, :, cols(kv)] for page in pages], axis=0)
            values = jnp.concatenate([vc_ref[page, :, cols(kv)] for page in pages], axis=0)
            values = jnp.concatenate([values, ones], axis=1)
            for head in range(kv * per_kv, (kv + 1) * per_kv):
                for chunk in range(ADDED_TOKENS // ROW_CHUNK):
                    rows = slice(chunk * ROW_CHUNK, (chunk + 1) * ROW_CHUNK)
                    scores = dot_nt(q_ref[rows, cols(head)], keys) + bias
                    old = m_ref[head, rows, :]
                    new = jnp.maximum(old, jnp.max(scores, axis=1, keepdims=True))
                    weights = jnp.exp2(
                        (scores - jnp.tile(new, (1, STEP_PAGES))) * EXP2_SCALE
                    ).astype(jnp.bfloat16)
                    keep = jnp.exp2((old - new) * EXP2_SCALE)
                    m_ref[head, rows, :] = new
                    acc_ref[head, rows, :] = acc_ref[head, rows, :] * jnp.tile(
                        keep, (1, 2)
                    ) + jnp.dot(weights, values, preferred_element_type=jnp.float32)
        return carry

    lax.fori_loop(0, (counts[request] + STEP_PAGES - 1) // STEP_PAGES, step, 0)
    eye = lax.broadcasted_iota(jnp.int32, (128, 128), 0) == lax.broadcasted_iota(
        jnp.int32, (128, 128), 1
    )
    for head in range(heads):
        den = jnp.maximum(acc_ref[head, :, HEAD_DIM:], 1.0)
        o_ref[head] = (acc_ref[head, :, :HEAD_DIM] / den).astype(jnp.bfloat16)
        scale = m_ref[head] * SCORE_SCALE + jnp.log(den)
        for block in range(ADDED_TOKENS // 128):
            part = scale[block * 128 : (block + 1) * 128]
            ls_ref[0, head : head + 1, block * 128 : (block + 1) * 128] = jnp.sum(
                jnp.where(eye, part, 0.0), axis=0, keepdims=True
            )


def attend(entries, counts, meta, gathered, key_cache, value_cache, per_kv, tok_rows):
    total_rows = gathered.shape[0]
    requests = total_rows // ADDED_TOKENS
    kv_cols = key_cache.shape[2]
    heads = kv_cols // HEAD_DIM * per_kv
    q_cols = heads * HEAD_DIM
    whole = pl.BlockSpec(
        key_cache.shape, lambda r, e, c, m: (0, 0, 0), pipeline_mode=pl.Buffered(1)
    )
    pages = key_cache.shape[0]
    return pl.pallas_call(
        functools.partial(attend_kernel, per_kv, tok_rows),
        out_shape=(
            jax.ShapeDtypeStruct((heads, total_rows, HEAD_DIM), jnp.bfloat16),
            jax.ShapeDtypeStruct((requests, heads, ADDED_TOKENS), jnp.float32),
        ),
        grid_spec=pltpu.PrefetchScalarGridSpec(
            num_scalar_prefetch=3,
            grid=(requests,),
            in_specs=[
                pl.BlockSpec((ADDED_TOKENS, q_cols), lambda r, e, c, m: (r, 0)),
                pl.BlockSpec((ADDED_TOKENS, kv_cols), lambda r, e, c, m: (m[0], q_cols // kv_cols)),
                pl.BlockSpec(
                    (ADDED_TOKENS, kv_cols), lambda r, e, c, m: (m[0], q_cols // kv_cols + 1)
                ),
                whole,
                whole,
            ],
            out_specs=(
                pl.BlockSpec((heads, ADDED_TOKENS, HEAD_DIM), lambda r, e, c, m: (0, r, 0)),
                pl.BlockSpec((1, heads, ADDED_TOKENS), lambda r, e, c, m: (r, 0, 0)),
            ),
            scratch_shapes=[
                pltpu.VMEM((heads, ADDED_TOKENS, HEAD_DIM), jnp.float32),
                pltpu.VMEM((heads, ADDED_TOKENS, 2 * HEAD_DIM), jnp.float32),
            ],
        ),
        compiler_params=pltpu.CompilerParams(
            dimension_semantics=("arbitrary",), vmem_limit_bytes=48 << 20
        ),
        cost_estimate=pl.CostEstimate(
            flops=4 * pages * PAGE_ROWS * ADDED_TOKENS * q_cols,
            bytes_accessed=4 * pages * PAGE_ROWS * kv_cols,
            transcendentals=pages * PAGE_ROWS * ADDED_TOKENS * heads,
        ),
    )(entries, counts, meta, gathered, gathered, gathered, key_cache, value_cache)


def page_lists(cached_lengths, group_ids, prompt_pages, own_pages, pages_dev, seq_index):
    own_len = cached_lengths - PROMPT_PAGES * PAGE_ROWS
    onehot = (group_ids[:, None] == jnp.arange(GROUPS, dtype=jnp.int32)[None, :]).astype(jnp.int32)
    request_prompt = jnp.sum(onehot[:, :, None] * prompt_pages[None, :, :], axis=1)
    slots = jnp.concatenate([request_prompt, own_pages], axis=1)
    count = slots.shape[1]
    position = jnp.arange(count, dtype=jnp.int32)
    live = jnp.where(
        position[None, :] < PROMPT_PAGES,
        PAGE_ROWS,
        jnp.clip(own_len[:, None] - (position[None, :] - PROMPT_PAGES) * PAGE_ROWS, 0, PAGE_ROWS),
    )
    owned = (slots // pages_dev == seq_index) & (live > 0)
    marks = owned.astype(jnp.int32)
    before = jnp.sum(
        jnp.where(position[None, None, :] < position[None, :, None], marks[:, None, :], 0), axis=2
    )
    packed = (slots - seq_index * pages_dev) * 256 + live
    length = -(-pages_dev // STEP_PAGES) * STEP_PAGES
    places = jnp.arange(length, dtype=jnp.int32)
    entries = jnp.sum(
        jnp.where(
            owned[:, None, :] & (before[:, None, :] == places[None, :, None]),
            packed[:, None, :],
            0,
        ),
        axis=2,
    )
    return entries, jnp.sum(marks, axis=1)


def body(
    hidden_in,
    norm_gain,
    query_weight,
    key_weight,
    value_weight,
    out_weight,
    key_cache,
    value_cache,
    cached_lengths,
    group_ids,
    prompt_pages,
    own_pages,
):
    tok_rows = hidden_in.shape[0]
    seq_count = lax.axis_size("seq")
    seq_index = lax.axis_index("seq")
    heads_dev = query_weight.shape[1] // HEAD_DIM
    kv_dev = key_weight.shape[1] // HEAD_DIM
    per_kv = heads_dev // kv_dev
    floats = hidden_in.astype(jnp.float32)
    normed = (
        floats * lax.rsqrt(jnp.mean(floats * floats, axis=-1, keepdims=True) + 1e-05) * norm_gain
    ).astype(jnp.bfloat16)
    projected = [
        jnp.dot(normed, weight, preferred_element_type=jnp.float32).astype(jnp.bfloat16)
        for weight in (query_weight, key_weight, value_weight)
    ]
    gathered = lax.all_gather(jnp.concatenate(projected, axis=1), "seq", axis=0, tiled=True)
    entries, counts = page_lists(
        cached_lengths, group_ids, prompt_pages, own_pages, key_cache.shape[0], seq_index
    )
    my_start = seq_index * tok_rows
    home = my_start // ADDED_TOKENS
    meta = jnp.stack([home, my_start - home * ADDED_TOKENS]).astype(jnp.int32)
    partial_value, log_scale = attend(
        entries, counts, meta, gathered, key_cache, value_cache, per_kv, tok_rows
    )
    log_scale = log_scale.transpose(1, 0, 2)
    got_part = lax.all_to_all(
        partial_value.reshape(heads_dev, seq_count, tok_rows, HEAD_DIM),
        "seq",
        split_axis=1,
        concat_axis=1,
        tiled=True,
    )
    got_scale = lax.all_to_all(
        log_scale.reshape(heads_dev, seq_count, tok_rows),
        "seq",
        split_axis=1,
        concat_axis=1,
        tiled=True,
    )
    highest = jnp.max(got_scale, axis=1)
    scale_weights = jnp.exp(got_scale - highest[:, None])
    attention = (
        jnp.sum(got_part.astype(jnp.float32) * scale_weights[..., None], axis=1)
        / jnp.sum(scale_weights, axis=1)[..., None]
    )
    attention = (
        attention.transpose(1, 0, 2).reshape(tok_rows, heads_dev * HEAD_DIM).astype(jnp.bfloat16)
    )
    head_terms = jnp.dot(attention, out_weight, preferred_element_type=jnp.float32)
    return lax.psum_scatter(head_terms, "tensor", scatter_dimension=1, tiled=True).astype(
        jnp.bfloat16
    )


def solution(mesh):
    in_specs = (
        P("seq", None),
        P(),
        P(None, "tensor"),
        P(None, "tensor"),
        P(None, "tensor"),
        P("tensor", None),
        P("seq", None, "tensor"),
        P("seq", None, "tensor"),
        P(),
        P(),
        P(),
        P(),
    )
    out_specs = P("seq", "tensor")
    return jax.shard_map(body, mesh=mesh, in_specs=in_specs, out_specs=out_specs, check_vma=False)
```

```python
import functools
import math

import jax
import jax.numpy as jnp
from jax import lax
from jax.experimental import pallas as pl
from jax.experimental.pallas import tpu as pltpu
from jax.sharding import PartitionSpec as P

HEAD_DIM = 128
PAGE_ROWS = 128
ADDED_TOKENS = 512
GROUPS = 2
PROMPT_PAGES = 128
STEP_PAGES = 4
ROW_CHUNK = 256
SCORE_SCALE = 1.0 / math.sqrt(HEAD_DIM)
EXP2_SCALE = SCORE_SCALE * math.log2(math.e)
EMPTY = -1e30
LINES = 8
MESH = pl.DeviceIdType.MESH


def dot_nt(left, right):
    return lax.dot_general(
        left, right, (((1,), (1,)), ((), ())), preferred_element_type=jnp.float32
    )


def attend_kernel(
    per_kv,
    tok_rows,
    entries,
    counts,
    meta,
    q_ref,
    kn_ref,
    vn_ref,
    kc_ref,
    vc_ref,
    o_ref,
    ls_ref,
    m_ref,
    acc_ref,
):
    request = pl.program_id(0)
    heads = m_ref.shape[0]
    kv_count = heads // per_kv
    ls_ref[...] = jnp.zeros_like(ls_ref)
    m_ref[...] = jnp.full_like(m_ref, EMPTY)
    acc_ref[...] = jnp.zeros_like(acc_ref)

    def cols(index):
        return slice(index * HEAD_DIM, (index + 1) * HEAD_DIM)

    @pl.when(meta[0] == request)
    def _():
        start = pl.multiple_of(meta[1], tok_rows)
        row = lax.broadcasted_iota(jnp.int32, (tok_rows, ADDED_TOKENS), 0)
        col = lax.broadcasted_iota(jnp.int32, (tok_rows, ADDED_TOKENS), 1)
        live = col <= row + start
        ones = jnp.ones((ADDED_TOKENS, HEAD_DIM), jnp.bfloat16)
        for head in range(heads):
            kv = head // per_kv
            scores = dot_nt(q_ref[pl.ds(start, tok_rows), cols(head)], kn_ref[:, cols(kv)])
            scores = jnp.where(live, scores, EMPTY)
            top = jnp.max(scores, axis=1, keepdims=True)
            weights = jnp.exp2((scores - top) * EXP2_SCALE).astype(jnp.bfloat16)
            values = jnp.concatenate([vn_ref[:, cols(kv)], ones], axis=1)
            m_ref[head, pl.ds(start, tok_rows), :] = jnp.broadcast_to(top, (tok_rows, HEAD_DIM))
            acc_ref[head, pl.ds(start, tok_rows), :] = jnp.dot(
                weights, values, preferred_element_type=jnp.float32
            )

    def step(index, carry):
        picked = [entries[request, index * STEP_PAGES + j] for j in range(STEP_PAGES)]
        lane = lax.broadcasted_iota(jnp.int32, (1, PAGE_ROWS), 1)
        bias = jnp.concatenate(
            [jnp.where(lane < (item & 255), 0.0, EMPTY) for item in picked], axis=1
        )
        pages = [item >> 8 for item in picked]
        ones = jnp.ones((STEP_PAGES * PAGE_ROWS, HEAD_DIM), jnp.bfloat16)
        for kv in range(kv_count):
            keys = jnp.concatenate([kc_ref[page, :, cols(kv)] for page in pages], axis=0)
            values = jnp.concatenate([vc_ref[page, :, cols(kv)] for page in pages], axis=0)
            values = jnp.concatenate([values, ones], axis=1)
            for head in range(kv * per_kv, (kv + 1) * per_kv):
                for chunk in range(ADDED_TOKENS // ROW_CHUNK):
                    rows = slice(chunk * ROW_CHUNK, (chunk + 1) * ROW_CHUNK)
                    scores = dot_nt(q_ref[rows, cols(head)], keys) + bias
                    old = m_ref[head, rows, :]
                    new = jnp.maximum(old, jnp.max(scores, axis=1, keepdims=True))
                    weights = jnp.exp2(
                        (scores - jnp.tile(new, (1, STEP_PAGES))) * EXP2_SCALE
                    ).astype(jnp.bfloat16)
                    keep = jnp.exp2((old - new) * EXP2_SCALE)
                    m_ref[head, rows, :] = new
                    acc_ref[head, rows, :] = acc_ref[head, rows, :] * jnp.tile(
                        keep, (1, 2)
                    ) + jnp.dot(weights, values, preferred_element_type=jnp.float32)
        return carry

    lax.fori_loop(0, (counts[request] + STEP_PAGES - 1) // STEP_PAGES, step, 0)
    eye = lax.broadcasted_iota(jnp.int32, (128, 128), 0) == lax.broadcasted_iota(
        jnp.int32, (128, 128), 1
    )
    for head in range(heads):
        den = jnp.maximum(acc_ref[head, :, HEAD_DIM:], 1.0)
        o_ref[:, cols(head)] = (acc_ref[head, :, :HEAD_DIM] / den).astype(jnp.bfloat16)
        scale = m_ref[head] * SCORE_SCALE + jnp.log(den)
        for block in range(ADDED_TOKENS // 128):
            part = scale[block * 128 : (block + 1) * 128]
            line = jnp.sum(jnp.where(eye, part, 0.0), axis=0, keepdims=True)
            for piece in range(128 // tok_rows):
                ls_ref[block * (128 // tok_rows) + piece, head : head + 1, :] = line[
                    :, piece * tok_rows : (piece + 1) * tok_rows
                ]


def attend(entries, counts, meta, queries, fresh, key_cache, value_cache, per_kv, tok_rows):
    total_rows = queries.shape[0]
    requests = total_rows // ADDED_TOKENS
    kv_cols = key_cache.shape[2]
    heads = kv_cols // HEAD_DIM * per_kv
    q_cols = heads * HEAD_DIM
    whole = pl.BlockSpec(
        key_cache.shape, lambda r, e, c, m: (0, 0, 0), pipeline_mode=pl.Buffered(1)
    )
    pages = key_cache.shape[0]
    return pl.pallas_call(
        functools.partial(attend_kernel, per_kv, tok_rows),
        out_shape=(
            jax.ShapeDtypeStruct((total_rows, q_cols), jnp.bfloat16),
            jax.ShapeDtypeStruct((total_rows // tok_rows, LINES, tok_rows), jnp.float32),
        ),
        grid_spec=pltpu.PrefetchScalarGridSpec(
            num_scalar_prefetch=3,
            grid=(requests,),
            in_specs=[
                pl.BlockSpec((ADDED_TOKENS, q_cols), lambda r, e, c, m: (r, 0)),
                pl.BlockSpec((ADDED_TOKENS, kv_cols), lambda r, e, c, m: (0, 0)),
                pl.BlockSpec((ADDED_TOKENS, kv_cols), lambda r, e, c, m: (0, 1)),
                whole,
                whole,
            ],
            out_specs=(
                pl.BlockSpec((ADDED_TOKENS, q_cols), lambda r, e, c, m: (r, 0)),
                pl.BlockSpec(
                    (ADDED_TOKENS // tok_rows, LINES, tok_rows), lambda r, e, c, m: (r, 0, 0)
                ),
            ),
            scratch_shapes=[
                pltpu.VMEM((heads, ADDED_TOKENS, HEAD_DIM), jnp.float32),
                pltpu.VMEM((heads, ADDED_TOKENS, 2 * HEAD_DIM), jnp.float32),
            ],
        ),
        compiler_params=pltpu.CompilerParams(
            dimension_semantics=("arbitrary",), vmem_limit_bytes=48 << 20
        ),
        cost_estimate=pl.CostEstimate(
            flops=4 * pages * PAGE_ROWS * ADDED_TOKENS * q_cols,
            bytes_accessed=4 * pages * PAGE_ROWS * kv_cols,
            transcendentals=pages * PAGE_ROWS * ADDED_TOKENS * heads,
        ),
    )(entries, counts, meta, queries, fresh, fresh, key_cache, value_cache)


def page_lists(cached_lengths, group_ids, prompt_pages, own_pages, pages_dev, seq_index):
    own_len = cached_lengths - PROMPT_PAGES * PAGE_ROWS
    onehot = (group_ids[:, None] == jnp.arange(GROUPS, dtype=jnp.int32)[None, :]).astype(jnp.int32)
    request_prompt = jnp.sum(onehot[:, :, None] * prompt_pages[None, :, :], axis=1)
    slots = jnp.concatenate([request_prompt, own_pages], axis=1)
    count = slots.shape[1]
    position = jnp.arange(count, dtype=jnp.int32)
    live = jnp.where(
        position[None, :] < PROMPT_PAGES,
        PAGE_ROWS,
        jnp.clip(own_len[:, None] - (position[None, :] - PROMPT_PAGES) * PAGE_ROWS, 0, PAGE_ROWS),
    )
    owned = (slots // pages_dev == seq_index) & (live > 0)
    marks = owned.astype(jnp.int32)
    before = jnp.sum(
        jnp.where(position[None, None, :] < position[None, :, None], marks[:, None, :], 0), axis=2
    )
    packed = (slots - seq_index * pages_dev) * 256 + live
    length = -(-pages_dev // STEP_PAGES) * STEP_PAGES
    places = jnp.arange(length, dtype=jnp.int32)
    entries = jnp.sum(
        jnp.where(
            owned[:, None, :] & (before[:, None, :] == places[None, :, None]),
            packed[:, None, :],
            0,
        ),
        axis=2,
    )
    return entries, jnp.sum(marks, axis=1)


def greet(peers):
    barrier = pltpu.get_barrier_semaphore()
    for peer in peers:
        pl.semaphore_signal(barrier, inc=1, device_id=peer, device_id_type=MESH)
    pl.semaphore_wait(barrier, len(peers))


def remote(source, target, send_sem, recv_sem, peer):
    return pltpu.make_async_remote_copy(
        src_ref=source,
        dst_ref=target,
        send_sem=send_sem,
        recv_sem=recv_sem,
        device_id=peer,
        device_id_type=MESH,
    )


def gather_kernel(
    seq_count,
    x_ref,
    gain_ref,
    wq_ref,
    wk_ref,
    wv_ref,
    q_ref,
    kv_ref,
    q_send,
    q_recv,
    qy_send,
    qy_recv,
    kv_send,
    kv_recv,
    kvy_send,
    kvy_recv,
):
    tok_rows = x_ref.shape[0]
    kv_cols = wk_ref.shape[1]
    me = lax.axis_index("seq")
    tensor = lax.axis_index("tensor")
    outer = seq_count // 2
    span = outer * ADDED_TOKENS // q_ref.shape[0]
    place, side = me // 2, me % 2
    base, inside = (place // span) * span, place % span
    twin = (place * 2 + 1 - side, tensor)

    def line_peer(distance):
        return (place + distance) % outer * 2 + side

    def span_peer(distance):
        return (base + (inside + distance) % span) * 2 + side

    def q_rows(owner):
        return pl.ds(pl.multiple_of(owner * tok_rows, tok_rows), tok_rows)

    def kv_rows(owner):
        local = owner - base * 2
        return pl.ds(pl.multiple_of(local * tok_rows, tok_rows), tok_rows)

    greet([twin] + [(line_peer(distance), tensor) for distance in range(1, outer)])

    floats = x_ref[...].astype(jnp.float32)
    mean = jnp.mean(floats * floats, axis=-1, keepdims=True)
    normed = (floats * lax.rsqrt(mean + 1e-05) * gain_ref[...]).astype(jnp.bfloat16)

    mine = q_rows(me)
    q_ref[mine, :] = jnp.dot(normed, wq_ref[...], preferred_element_type=jnp.float32).astype(
        jnp.bfloat16
    )
    started = []
    own = q_ref.at[mine, :]
    for distance in range(1, outer):
        peer = (line_peer(distance), tensor)
        copy = remote(own, own, q_send.at[distance], q_recv.at[distance], peer)
        copy.start()
        started.append(copy)
    copy = remote(own, own, qy_send.at[0], qy_recv.at[0], twin)
    copy.start()
    started.append(copy)

    mine = kv_rows(me)
    for start, weight in ((0, wk_ref), (kv_cols, wv_ref)):
        kv_ref[mine, start : start + kv_cols] = jnp.dot(
            normed, weight[...], preferred_element_type=jnp.float32
        ).astype(jnp.bfloat16)
    own = kv_ref.at[mine, :]
    for distance in range(1, span):
        peer = (span_peer(distance), tensor)
        copy = remote(own, own, kv_send.at[distance], kv_recv.at[distance], peer)
        copy.start()
        started.append(copy)
    copy = remote(own, own, kvy_send.at[0], kvy_recv.at[0], twin)
    copy.start()
    started.append(copy)

    late = []
    for distance in range(1, outer):
        owner = line_peer(outer - distance)
        block = q_ref.at[q_rows(owner), :]
        remote(block, block, q_send.at[distance], q_recv.at[distance], twin).wait_recv()
        copy = remote(block, block, qy_send.at[distance], qy_recv.at[distance], twin)
        copy.start()
        started.append(copy)
        if distance < span:
            owner = span_peer(span - distance)
            block = kv_ref.at[kv_rows(owner), :]
            remote(block, block, kv_send.at[distance], kv_recv.at[distance], twin).wait_recv()
            copy = remote(block, block, kvy_send.at[distance], kvy_recv.at[distance], twin)
            copy.start()
            started.append(copy)
    for distance in range(outer):
        owner = (place + outer - distance) % outer * 2 + 1 - side
        block = q_ref.at[q_rows(owner), :]
        late.append(remote(block, block, qy_send.at[distance], qy_recv.at[distance], twin))
    for distance in range(span):
        owner = (base + (inside + span - distance) % span) * 2 + 1 - side
        block = kv_ref.at[kv_rows(owner), :]
        late.append(remote(block, block, kvy_send.at[distance], kvy_recv.at[distance], twin))
    for copy in late:
        copy.wait_recv()
    for copy in started:
        copy.wait_send()


def gather(hidden_in, norm_gain, query_weight, key_weight, value_weight, seq_count):
    tok_rows = hidden_in.shape[0]
    q_cols, kv_cols = query_weight.shape[1], key_weight.shape[1]
    slots = pltpu.SemaphoreType.DMA((seq_count // 2,))
    vmem = pl.BlockSpec(memory_space=pltpu.VMEM)
    return pl.pallas_call(
        functools.partial(gather_kernel, seq_count),
        out_shape=(
            jax.ShapeDtypeStruct((tok_rows * seq_count, q_cols), jnp.bfloat16),
            jax.ShapeDtypeStruct((ADDED_TOKENS, 2 * kv_cols), jnp.bfloat16),
        ),
        in_specs=[vmem] * 5,
        out_specs=(vmem, vmem),
        scratch_shapes=[slots] * 8,
        compiler_params=pltpu.CompilerParams(
            collective_id=0, has_side_effects=True, vmem_limit_bytes=24 << 20
        ),
    )(hidden_in, norm_gain.reshape(1, -1), query_weight, key_weight, value_weight)


def finish_kernel(
    seq_count,
    tensor_count,
    part_ref,
    ls_ref,
    w_ref,
    out_ref,
    got_ref,
    gls_ref,
    near_ref,
    near_got,
    far_ref,
    far_got,
    part_send,
    part_recv,
    ls_send,
    ls_recv,
    near_send,
    near_recv,
    far_send,
    far_recv,
):
    tok_rows, out_cols = out_ref.shape
    heads = part_ref.shape[1] // HEAD_DIM
    me = lax.axis_index("seq")
    tensor = lax.axis_index("tensor")
    pair, core = tensor // 2, tensor % 2
    pairs = tensor_count // 2
    twin = (me, pair * 2 + 1 - core)

    def far_pair(distance):
        return (pair + distance) % pairs

    def seq_peer(distance):
        return (me + distance) % seq_count

    greet(
        [(seq_peer(distance), tensor) for distance in range(1, seq_count)]
        + [twin]
        + [(me, far_pair(distance) * 2 + core) for distance in range(1, pairs)]
    )
    scales, parts = [], []
    for distance in range(1, seq_count):
        owner = seq_peer(distance)
        copy = remote(
            ls_ref.at[owner],
            gls_ref.at[distance],
            ls_send.at[distance],
            ls_recv.at[distance],
            (owner, tensor),
        )
        copy.start()
        scales.append(copy)
    for distance in range(1, seq_count):
        owner = seq_peer(distance)
        copy = remote(
            part_ref.at[pl.ds(pl.multiple_of(owner * tok_rows, tok_rows), tok_rows), :],
            got_ref.at[distance],
            part_send.at[distance],
            part_recv.at[distance],
            (owner, tensor),
        )
        copy.start()
        parts.append(copy)
    gls_ref[0] = ls_ref[me]
    for copy in scales:
        copy.wait_recv()
    lines = gls_ref[...]
    lines = jnp.exp(lines - jnp.max(lines, axis=0, keepdims=True))
    lines = lines / jnp.sum(lines, axis=0, keepdims=True)
    eye = (
        lax.broadcasted_iota(jnp.int32, (tok_rows, tok_rows), 0)
        == lax.broadcasted_iota(jnp.int32, (tok_rows, tok_rows), 1)
    ).astype(jnp.float32)
    shares = lax.dot_general(
        eye,
        lines.reshape(seq_count * LINES, tok_rows),
        (((1,), (1,)), ((), ())),
        precision=lax.Precision.HIGHEST,
        preferred_element_type=jnp.float32,
    )

    def weighted(block, distance):
        return [
            block[:, head * HEAD_DIM : (head + 1) * HEAD_DIM].astype(jnp.float32)
            * shares[:, distance * LINES + head : distance * LINES + head + 1]
            for head in range(heads)
        ]

    mine = pl.ds(pl.multiple_of(me * tok_rows, tok_rows), tok_rows)
    total = weighted(part_ref[mine, :], 0)
    for distance in range(1, seq_count):
        parts[distance - 1].wait_recv()
        terms = weighted(got_ref[distance], distance)
        total = [left + right for left, right in zip(total, terms)]
    attention = jnp.concatenate(total, axis=1).astype(jnp.bfloat16)

    def terms_for(owner):
        start = pl.multiple_of(owner * out_cols, out_cols)
        return jnp.dot(
            attention, w_ref[:, pl.ds(start, out_cols)], preferred_element_type=jnp.float32
        )

    started = []
    nears = []
    for distance in list(range(1, pairs)) + [0]:
        near_ref[distance] = terms_for(far_pair(distance) * 2 + 1 - core)
        copy = remote(
            near_ref.at[distance],
            near_got.at[distance],
            near_send.at[distance],
            near_recv.at[distance],
            twin,
        )
        copy.start()
        started.append(copy)
        nears.append((distance, copy))
    fars = []
    for distance, copy in nears[:-1]:
        owner = far_pair(distance) * 2 + core
        terms = terms_for(owner)
        copy.wait_recv()
        far_ref[distance] = terms + near_got[distance]
        copy = remote(
            far_ref.at[distance],
            far_got.at[distance],
            far_send.at[distance],
            far_recv.at[distance],
            (me, owner),
        )
        copy.start()
        started.append(copy)
        fars.append(copy)
    result = terms_for(tensor)
    nears[-1][1].wait_recv()
    result = result + near_got[0]
    for distance in range(1, pairs):
        fars[distance - 1].wait_recv()
        result = result + far_got[distance]
    out_ref[...] = result.astype(jnp.bfloat16)
    for copy in scales + parts + started:
        copy.wait_send()


def finish(partial_value, log_scale, out_weight, seq_count, tensor_count):
    tok_rows = partial_value.shape[0] // seq_count
    out_cols = out_weight.shape[1] // tensor_count
    pairs = tensor_count // 2
    vmem = pl.BlockSpec(memory_space=pltpu.VMEM)
    block = pltpu.VMEM((pairs, tok_rows, out_cols), jnp.float32)
    seq_sems = pltpu.SemaphoreType.DMA((seq_count,))
    pair_sems = pltpu.SemaphoreType.DMA((pairs,))
    return pl.pallas_call(
        functools.partial(finish_kernel, seq_count, tensor_count),
        out_shape=jax.ShapeDtypeStruct((tok_rows, out_cols), jnp.bfloat16),
        in_specs=[vmem] * 3,
        out_specs=vmem,
        scratch_shapes=[
            pltpu.VMEM((seq_count, tok_rows, partial_value.shape[1]), jnp.bfloat16),
            pltpu.VMEM((seq_count, LINES, tok_rows), jnp.float32),
            block,
            block,
            block,
            block,
        ]
        + [seq_sems] * 4
        + [pair_sems] * 4,
        compiler_params=pltpu.CompilerParams(
            collective_id=1, has_side_effects=True, vmem_limit_bytes=24 << 20
        ),
    )(partial_value, log_scale, out_weight)


def body(
    hidden_in,
    norm_gain,
    query_weight,
    key_weight,
    value_weight,
    out_weight,
    key_cache,
    value_cache,
    cached_lengths,
    group_ids,
    prompt_pages,
    own_pages,
):
    tok_rows = hidden_in.shape[0]
    seq_count = lax.axis_size("seq")
    seq_index = lax.axis_index("seq")
    heads_dev = query_weight.shape[1] // HEAD_DIM
    kv_dev = key_weight.shape[1] // HEAD_DIM
    per_kv = heads_dev // kv_dev
    queries, fresh = gather(
        hidden_in, norm_gain, query_weight, key_weight, value_weight, seq_count
    )
    entries, counts = page_lists(
        cached_lengths, group_ids, prompt_pages, own_pages, key_cache.shape[0], seq_index
    )
    my_start = seq_index * tok_rows
    home = my_start // ADDED_TOKENS
    meta = jnp.stack([home, my_start - home * ADDED_TOKENS]).astype(jnp.int32)
    partial_value, log_scale = attend(
        entries, counts, meta, queries, fresh, key_cache, value_cache, per_kv, tok_rows
    )
    return finish(partial_value, log_scale, out_weight, seq_count, lax.axis_size("tensor"))


def solution(mesh):
    in_specs = (
        P("seq", None),
        P(),
        P(None, "tensor"),
        P(None, "tensor"),
        P(None, "tensor"),
        P("tensor", None),
        P("seq", None, "tensor"),
        P("seq", None, "tensor"),
        P(),
        P(),
        P(),
        P(),
    )
    out_specs = P("seq", "tensor")
    return jax.shard_map(body, mesh=mesh, in_specs=in_specs, out_specs=out_specs, check_vma=False)
```

```python
import functools
import math

import jax
import jax.numpy as jnp
from jax import lax
from jax.experimental import pallas as pl
from jax.experimental.pallas import tpu as pltpu
from jax.sharding import PartitionSpec as P

HEAD_DIM = 128
PAGE_ROWS = 128
ADDED_TOKENS = 512
GROUPS = 2
PROMPT_PAGES = 128
STEP_PAGES = 4
ROW_CHUNK = 256
SCORE_SCALE = 1.0 / math.sqrt(HEAD_DIM)
EXP2_SCALE = SCORE_SCALE * math.log2(math.e)
EMPTY = -1e30
LINES = 8
MESH = pl.DeviceIdType.MESH


def dot_nt(left, right):
    return lax.dot_general(
        left, right, (((1,), (1,)), ((), ())), preferred_element_type=jnp.float32
    )


def attend_kernel(
    per_kv,
    tok_rows,
    entries,
    counts,
    meta,
    q_ref,
    kn_ref,
    vn_ref,
    kc_ref,
    vc_ref,
    o_ref,
    ls_ref,
    m_ref,
    acc_ref,
):
    request = pl.program_id(0)
    heads = m_ref.shape[0]
    kv_count = heads // per_kv
    ls_ref[...] = jnp.zeros_like(ls_ref)
    m_ref[...] = jnp.full_like(m_ref, EMPTY)
    acc_ref[...] = jnp.zeros_like(acc_ref)

    def cols(index):
        return slice(index * HEAD_DIM, (index + 1) * HEAD_DIM)

    @pl.when(meta[0] == request)
    def _():
        start = pl.multiple_of(meta[1], tok_rows)
        row = lax.broadcasted_iota(jnp.int32, (tok_rows, ADDED_TOKENS), 0)
        col = lax.broadcasted_iota(jnp.int32, (tok_rows, ADDED_TOKENS), 1)
        live = col <= row + start
        ones = jnp.ones((ADDED_TOKENS, HEAD_DIM), jnp.bfloat16)
        for head in range(heads):
            kv = head // per_kv
            scores = dot_nt(q_ref[pl.ds(start, tok_rows), cols(head)], kn_ref[:, cols(kv)])
            scores = jnp.where(live, scores, EMPTY)
            top = jnp.max(scores, axis=1, keepdims=True)
            weights = jnp.exp2((scores - top) * EXP2_SCALE).astype(jnp.bfloat16)
            values = jnp.concatenate([vn_ref[:, cols(kv)], ones], axis=1)
            m_ref[head, pl.ds(start, tok_rows), :] = jnp.broadcast_to(top, (tok_rows, HEAD_DIM))
            acc_ref[head, pl.ds(start, tok_rows), :] = jnp.dot(
                weights, values, preferred_element_type=jnp.float32
            )

    def step(index, carry):
        picked = [entries[request, index * STEP_PAGES + j] for j in range(STEP_PAGES)]
        lane = lax.broadcasted_iota(jnp.int32, (1, PAGE_ROWS), 1)
        bias = jnp.concatenate(
            [jnp.where(lane < (item & 255), 0.0, EMPTY) for item in picked], axis=1
        )
        pages = [item >> 8 for item in picked]
        ones = jnp.ones((STEP_PAGES * PAGE_ROWS, HEAD_DIM), jnp.bfloat16)
        for kv in range(kv_count):
            keys = jnp.concatenate([kc_ref[page, :, cols(kv)] for page in pages], axis=0)
            values = jnp.concatenate([vc_ref[page, :, cols(kv)] for page in pages], axis=0)
            values = jnp.concatenate([values, ones], axis=1)
            for head in range(kv * per_kv, (kv + 1) * per_kv):
                for chunk in range(ADDED_TOKENS // ROW_CHUNK):
                    rows = slice(chunk * ROW_CHUNK, (chunk + 1) * ROW_CHUNK)
                    scores = dot_nt(q_ref[rows, cols(head)], keys) + bias
                    old = m_ref[head, rows, :]
                    new = jnp.maximum(old, jnp.max(scores, axis=1, keepdims=True))
                    weights = jnp.exp2(
                        (scores - jnp.tile(new, (1, STEP_PAGES))) * EXP2_SCALE
                    ).astype(jnp.bfloat16)
                    keep = jnp.exp2((old - new) * EXP2_SCALE)
                    m_ref[head, rows, :] = new
                    acc_ref[head, rows, :] = acc_ref[head, rows, :] * jnp.tile(
                        keep, (1, 2)
                    ) + jnp.dot(weights, values, preferred_element_type=jnp.float32)
        return carry

    lax.fori_loop(0, (counts[request] + STEP_PAGES - 1) // STEP_PAGES, step, 0)
    eye = lax.broadcasted_iota(jnp.int32, (128, 128), 0) == lax.broadcasted_iota(
        jnp.int32, (128, 128), 1
    )
    for head in range(heads):
        den = jnp.maximum(acc_ref[head, :, HEAD_DIM:], 1.0)
        o_ref[:, cols(head)] = (acc_ref[head, :, :HEAD_DIM] / den).astype(jnp.bfloat16)
        scale = m_ref[head] * SCORE_SCALE + jnp.log(den)
        for block in range(ADDED_TOKENS // 128):
            part = scale[block * 128 : (block + 1) * 128]
            line = jnp.sum(jnp.where(eye, part, 0.0), axis=0, keepdims=True)
            for piece in range(128 // tok_rows):
                ls_ref[block * (128 // tok_rows) + piece, head : head + 1, :] = line[
                    :, piece * tok_rows : (piece + 1) * tok_rows
                ]


def attend(entries, counts, meta, queries, fresh, key_cache, value_cache, per_kv, tok_rows):
    total_rows = queries.shape[0]
    requests = total_rows // ADDED_TOKENS
    kv_cols = key_cache.shape[2]
    heads = kv_cols // HEAD_DIM * per_kv
    q_cols = heads * HEAD_DIM
    whole = pl.BlockSpec(
        key_cache.shape, lambda r, e, c, m: (0, 0, 0), pipeline_mode=pl.Buffered(1)
    )
    pages = key_cache.shape[0]
    return pl.pallas_call(
        functools.partial(attend_kernel, per_kv, tok_rows),
        out_shape=(
            jax.ShapeDtypeStruct((total_rows, q_cols), jnp.bfloat16),
            jax.ShapeDtypeStruct((total_rows // tok_rows, LINES, tok_rows), jnp.float32),
        ),
        grid_spec=pltpu.PrefetchScalarGridSpec(
            num_scalar_prefetch=3,
            grid=(requests,),
            in_specs=[
                pl.BlockSpec((ADDED_TOKENS, q_cols), lambda r, e, c, m: (r, 0)),
                pl.BlockSpec((ADDED_TOKENS, kv_cols), lambda r, e, c, m: (0, 0)),
                pl.BlockSpec((ADDED_TOKENS, kv_cols), lambda r, e, c, m: (0, 1)),
                whole,
                whole,
            ],
            out_specs=(
                pl.BlockSpec((ADDED_TOKENS, q_cols), lambda r, e, c, m: (r, 0)),
                pl.BlockSpec(
                    (ADDED_TOKENS // tok_rows, LINES, tok_rows), lambda r, e, c, m: (r, 0, 0)
                ),
            ),
            scratch_shapes=[
                pltpu.VMEM((heads, ADDED_TOKENS, HEAD_DIM), jnp.float32),
                pltpu.VMEM((heads, ADDED_TOKENS, 2 * HEAD_DIM), jnp.float32),
            ],
        ),
        compiler_params=pltpu.CompilerParams(
            dimension_semantics=("arbitrary",), vmem_limit_bytes=48 << 20
        ),
        cost_estimate=pl.CostEstimate(
            flops=4 * pages * PAGE_ROWS * ADDED_TOKENS * q_cols,
            bytes_accessed=4 * pages * PAGE_ROWS * kv_cols,
            transcendentals=pages * PAGE_ROWS * ADDED_TOKENS * heads,
        ),
    )(entries, counts, meta, queries, fresh, fresh, key_cache, value_cache)


def page_lists(cached_lengths, group_ids, prompt_pages, own_pages, pages_dev, seq_index):
    own_len = cached_lengths - PROMPT_PAGES * PAGE_ROWS
    onehot = (group_ids[:, None] == jnp.arange(GROUPS, dtype=jnp.int32)[None, :]).astype(jnp.int32)
    request_prompt = jnp.sum(onehot[:, :, None] * prompt_pages[None, :, :], axis=1)
    slots = jnp.concatenate([request_prompt, own_pages], axis=1)
    count = slots.shape[1]
    position = jnp.arange(count, dtype=jnp.int32)
    live = jnp.where(
        position[None, :] < PROMPT_PAGES,
        PAGE_ROWS,
        jnp.clip(own_len[:, None] - (position[None, :] - PROMPT_PAGES) * PAGE_ROWS, 0, PAGE_ROWS),
    )
    owned = (slots // pages_dev == seq_index) & (live > 0)
    marks = owned.astype(jnp.int32)
    before = jnp.sum(
        jnp.where(position[None, None, :] < position[None, :, None], marks[:, None, :], 0), axis=2
    )
    packed = (slots - seq_index * pages_dev) * 256 + live
    length = -(-pages_dev // STEP_PAGES) * STEP_PAGES
    places = jnp.arange(length, dtype=jnp.int32)
    entries = jnp.sum(
        jnp.where(
            owned[:, None, :] & (before[:, None, :] == places[None, :, None]),
            packed[:, None, :],
            0,
        ),
        axis=2,
    )
    return entries, jnp.sum(marks, axis=1)


def greet(peers):
    barrier = pltpu.get_barrier_semaphore()
    for peer in peers:
        pl.semaphore_signal(barrier, inc=1, device_id=peer, device_id_type=MESH)
    pl.semaphore_wait(barrier, len(peers))


def remote(source, target, send_sem, recv_sem, peer):
    return pltpu.make_async_remote_copy(
        src_ref=source,
        dst_ref=target,
        send_sem=send_sem,
        recv_sem=recv_sem,
        device_id=peer,
        device_id_type=MESH,
    )


def gather_kernel(
    seq_count,
    x_ref,
    gain_ref,
    wq_ref,
    wk_ref,
    wv_ref,
    q_ref,
    kv_ref,
    q_send,
    q_recv,
    qy_send,
    qy_recv,
    kv_send,
    kv_recv,
    kvy_send,
    kvy_recv,
    wq_buf,
    wk_buf,
    wv_buf,
    load_sem,
):
    tok_rows = x_ref.shape[0]
    kv_cols = wk_ref.shape[1]
    loads = [
        pltpu.make_async_copy(source, target, load_sem.at[index])
        for index, (source, target) in enumerate(
            ((wq_ref, wq_buf), (wk_ref, wk_buf), (wv_ref, wv_buf))
        )
    ]
    for load in loads:
        load.start()
    me = lax.axis_index("seq")
    tensor = lax.axis_index("tensor")
    outer = seq_count // 2
    span = outer * ADDED_TOKENS // q_ref.shape[0]
    place, side = me // 2, me % 2
    base, inside = (place // span) * span, place % span
    twin = (place * 2 + 1 - side, tensor)

    def line_peer(distance):
        return (place + distance) % outer * 2 + side

    def span_peer(distance):
        return (base + (inside + distance) % span) * 2 + side

    def q_rows(owner):
        return pl.ds(pl.multiple_of(owner * tok_rows, tok_rows), tok_rows)

    def kv_rows(owner):
        local = owner - base * 2
        return pl.ds(pl.multiple_of(local * tok_rows, tok_rows), tok_rows)

    greet([twin] + [(line_peer(distance), tensor) for distance in range(1, outer)])

    floats = x_ref[...].astype(jnp.float32)
    mean = jnp.mean(floats * floats, axis=-1, keepdims=True)
    normed = (floats * lax.rsqrt(mean + 1e-05) * gain_ref[...]).astype(jnp.bfloat16)

    mine = q_rows(me)
    loads[0].wait()
    q_ref[mine, :] = jnp.dot(normed, wq_buf[...], preferred_element_type=jnp.float32).astype(
        jnp.bfloat16
    )
    started = []
    own = q_ref.at[mine, :]
    for distance in range(1, outer):
        peer = (line_peer(distance), tensor)
        copy = remote(own, own, q_send.at[distance], q_recv.at[distance], peer)
        copy.start()
        started.append(copy)
    copy = remote(own, own, qy_send.at[0], qy_recv.at[0], twin)
    copy.start()
    started.append(copy)

    mine = kv_rows(me)
    loads[1].wait()
    loads[2].wait()
    for start, weight in ((0, wk_buf), (kv_cols, wv_buf)):
        kv_ref[mine, start : start + kv_cols] = jnp.dot(
            normed, weight[...], preferred_element_type=jnp.float32
        ).astype(jnp.bfloat16)
    own = kv_ref.at[mine, :]
    for distance in range(1, span):
        peer = (span_peer(distance), tensor)
        copy = remote(own, own, kv_send.at[distance], kv_recv.at[distance], peer)
        copy.start()
        started.append(copy)
    copy = remote(own, own, kvy_send.at[0], kvy_recv.at[0], twin)
    copy.start()
    started.append(copy)

    late = []
    for distance in range(1, outer):
        owner = line_peer(outer - distance)
        block = q_ref.at[q_rows(owner), :]
        remote(block, block, q_send.at[distance], q_recv.at[distance], twin).wait_recv()
        copy = remote(block, block, qy_send.at[distance], qy_recv.at[distance], twin)
        copy.start()
        started.append(copy)
        if distance < span:
            owner = span_peer(span - distance)
            block = kv_ref.at[kv_rows(owner), :]
            remote(block, block, kv_send.at[distance], kv_recv.at[distance], twin).wait_recv()
            copy = remote(block, block, kvy_send.at[distance], kvy_recv.at[distance], twin)
            copy.start()
            started.append(copy)
    for distance in range(outer):
        owner = (place + outer - distance) % outer * 2 + 1 - side
        block = q_ref.at[q_rows(owner), :]
        late.append(remote(block, block, qy_send.at[distance], qy_recv.at[distance], twin))
    for distance in range(span):
        owner = (base + (inside + span - distance) % span) * 2 + 1 - side
        block = kv_ref.at[kv_rows(owner), :]
        late.append(remote(block, block, kvy_send.at[distance], kvy_recv.at[distance], twin))
    for copy in late:
        copy.wait_recv()
    for copy in started:
        copy.wait_send()


def gather(hidden_in, norm_gain, query_weight, key_weight, value_weight, seq_count):
    tok_rows = hidden_in.shape[0]
    q_cols, kv_cols = query_weight.shape[1], key_weight.shape[1]
    slots = pltpu.SemaphoreType.DMA((seq_count // 2,))
    vmem = pl.BlockSpec(memory_space=pltpu.VMEM)
    return pl.pallas_call(
        functools.partial(gather_kernel, seq_count),
        out_shape=(
            jax.ShapeDtypeStruct((tok_rows * seq_count, q_cols), jnp.bfloat16),
            jax.ShapeDtypeStruct((ADDED_TOKENS, 2 * kv_cols), jnp.bfloat16),
        ),
        in_specs=[vmem] * 2 + [pl.BlockSpec(memory_space=pltpu.HBM)] * 3,
        out_specs=(vmem, vmem),
        scratch_shapes=[slots] * 8
        + [
            pltpu.VMEM(weight.shape, weight.dtype)
            for weight in (query_weight, key_weight, value_weight)
        ]
        + [pltpu.SemaphoreType.DMA((3,))],
        compiler_params=pltpu.CompilerParams(
            collective_id=0, has_side_effects=True, vmem_limit_bytes=24 << 20
        ),
    )(hidden_in, norm_gain.reshape(1, -1), query_weight, key_weight, value_weight)


def finish_kernel(
    seq_count,
    tensor_count,
    part_ref,
    ls_ref,
    w_ref,
    out_ref,
    mix_ref,
    mix_got,
    mls_ref,
    side_got,
    sls_ref,
    gls_ref,
    near_ref,
    near_got,
    far_ref,
    far_got,
    side_send,
    side_recv,
    sls_send,
    sls_recv,
    mix_send,
    mix_recv,
    mls_send,
    mls_recv,
    near_send,
    near_recv,
    far_send,
    far_recv,
):
    tok_rows, out_cols = out_ref.shape
    heads = part_ref.shape[1] // HEAD_DIM
    me = lax.axis_index("seq")
    tensor = lax.axis_index("tensor")
    pair, core = tensor // 2, tensor % 2
    pairs = tensor_count // 2
    twin = (me, pair * 2 + 1 - core)
    outer = seq_count // 2
    place, side = me // 2, me % 2
    beside = (place * 2 + 1 - side, tensor)
    order = sorted(range(1, outer), key=lambda distance: -min(distance, outer - distance))

    def far_pair(distance):
        return (pair + distance) % pairs

    def line(distance, which):
        return (place + distance) % outer * 2 + which

    def rows(owner):
        return pl.ds(pl.multiple_of(owner * tok_rows, tok_rows), tok_rows)

    greet(
        [beside]
        + [(line(distance, side), tensor) for distance in range(1, outer)]
        + [twin]
        + [(me, far_pair(distance) * 2 + core) for distance in range(1, pairs)]
    )
    started = []
    scales, sides, mixes, mix_scales = {}, {}, {}, {}
    for distance in order + [0]:
        scales[distance] = remote(
            ls_ref.at[line(distance, 1 - side)],
            sls_ref.at[distance],
            sls_send.at[distance],
            sls_recv.at[distance],
            beside,
        )
        scales[distance].start()
    for distance in order + [0]:
        sides[distance] = remote(
            part_ref.at[rows(line(distance, 1 - side)), :],
            side_got.at[distance],
            side_send.at[distance],
            side_recv.at[distance],
            beside,
        )
        sides[distance].start()
    for distance in order + [0]:
        scales[distance].wait_recv()
    eye = (
        lax.broadcasted_iota(jnp.int32, (tok_rows, tok_rows), 0)
        == lax.broadcasted_iota(jnp.int32, (tok_rows, tok_rows), 1)
    ).astype(jnp.float32)

    def columns(lines):
        return lax.dot_general(
            eye,
            lines.reshape(-1, tok_rows),
            (((1,), (1,)), ((), ())),
            precision=lax.Precision.HIGHEST,
            preferred_element_type=jnp.float32,
        )

    def weighted(block, shares, index):
        return [
            block[:, head * HEAD_DIM : (head + 1) * HEAD_DIM].astype(jnp.float32)
            * shares[:, index * LINES + head : index * LINES + head + 1]
            for head in range(heads)
        ]

    def plus(left, right):
        return [one + other for one, other in zip(left, right)]

    own_lines = jnp.stack([ls_ref[line(distance, side)] for distance in range(outer)])
    side_lines = sls_ref[...]
    top = jnp.maximum(own_lines, side_lines)
    own_scale, side_scale = jnp.exp(own_lines - top), jnp.exp(side_lines - top)
    both = own_scale + side_scale
    mls_ref[...] = top + jnp.log(both)
    for distance in order:
        mix_scales[distance] = remote(
            mls_ref.at[distance],
            gls_ref.at[distance],
            mls_send.at[distance],
            mls_recv.at[distance],
            (line(distance, side), tensor),
        )
        mix_scales[distance].start()
    own_shares, side_shares = columns(own_scale / both), columns(side_scale / both)

    def mixed(distance):
        return plus(
            weighted(part_ref[rows(line(distance, side)), :], own_shares, distance),
            weighted(side_got[distance], side_shares, distance),
        )

    for distance in order:
        sides[distance].wait_recv()
        mix_ref[distance] = jnp.concatenate(mixed(distance), axis=1).astype(jnp.bfloat16)
        mixes[distance] = remote(
            mix_ref.at[distance],
            mix_got.at[distance],
            mix_send.at[distance],
            mix_recv.at[distance],
            (line(distance, side), tensor),
        )
        mixes[distance].start()
    gls_ref[0] = mls_ref[0]
    for distance in order:
        mix_scales[distance].wait_recv()
    lines = gls_ref[...]
    lines = jnp.exp(lines - jnp.max(lines, axis=0, keepdims=True))
    shares = columns(lines / jnp.sum(lines, axis=0, keepdims=True))
    sides[0].wait_recv()
    total = [
        block * shares[:, head : head + 1] for head, block in enumerate(mixed(0))
    ]
    for distance in order:
        mixes[distance].wait_recv()
        total = plus(total, weighted(mix_got[distance], shares, distance))
    for group in (scales, sides, mixes, mix_scales):
        started.extend(group.values())
    attention = jnp.concatenate(total, axis=1).astype(jnp.bfloat16)

    def terms_for(owner):
        start = pl.multiple_of(owner * out_cols, out_cols)
        return jnp.dot(
            attention, w_ref[:, pl.ds(start, out_cols)], preferred_element_type=jnp.float32
        )

    nears = []
    for distance in list(range(1, pairs)) + [0]:
        near_ref[distance] = terms_for(far_pair(distance) * 2 + 1 - core)
        copy = remote(
            near_ref.at[distance],
            near_got.at[distance],
            near_send.at[distance],
            near_recv.at[distance],
            twin,
        )
        copy.start()
        started.append(copy)
        nears.append((distance, copy))
    fars = []
    for distance, copy in nears[:-1]:
        owner = far_pair(distance) * 2 + core
        terms = terms_for(owner)
        copy.wait_recv()
        far_ref[distance] = terms + near_got[distance]
        copy = remote(
            far_ref.at[distance],
            far_got.at[distance],
            far_send.at[distance],
            far_recv.at[distance],
            (me, owner),
        )
        copy.start()
        started.append(copy)
        fars.append(copy)
    result = terms_for(tensor)
    nears[-1][1].wait_recv()
    result = result + near_got[0]
    for distance in range(1, pairs):
        fars[distance - 1].wait_recv()
        result = result + far_got[distance]
    out_ref[...] = result.astype(jnp.bfloat16)
    for copy in started:
        copy.wait_send()


def finish(partial_value, log_scale, out_weight, seq_count, tensor_count):
    tok_rows = partial_value.shape[0] // seq_count
    out_cols = out_weight.shape[1] // tensor_count
    pairs = tensor_count // 2
    vmem = pl.BlockSpec(memory_space=pltpu.VMEM)
    block = pltpu.VMEM((pairs, tok_rows, out_cols), jnp.float32)
    outer = seq_count // 2
    parts = pltpu.VMEM((outer, tok_rows, partial_value.shape[1]), jnp.bfloat16)
    scales = pltpu.VMEM((outer, LINES, tok_rows), jnp.float32)
    line_sems = pltpu.SemaphoreType.DMA((outer,))
    pair_sems = pltpu.SemaphoreType.DMA((pairs,))
    return pl.pallas_call(
        functools.partial(finish_kernel, seq_count, tensor_count),
        out_shape=jax.ShapeDtypeStruct((tok_rows, out_cols), jnp.bfloat16),
        in_specs=[vmem] * 3,
        out_specs=vmem,
        scratch_shapes=[
            parts,
            parts,
            scales,
            parts,
            scales,
            scales,
            block,
            block,
            block,
            block,
        ]
        + [line_sems] * 8
        + [pair_sems] * 4,
        compiler_params=pltpu.CompilerParams(
            collective_id=1, has_side_effects=True, vmem_limit_bytes=24 << 20
        ),
    )(partial_value, log_scale, out_weight)


def body(
    hidden_in,
    norm_gain,
    query_weight,
    key_weight,
    value_weight,
    out_weight,
    key_cache,
    value_cache,
    cached_lengths,
    group_ids,
    prompt_pages,
    own_pages,
):
    tok_rows = hidden_in.shape[0]
    seq_count = lax.axis_size("seq")
    seq_index = lax.axis_index("seq")
    heads_dev = query_weight.shape[1] // HEAD_DIM
    kv_dev = key_weight.shape[1] // HEAD_DIM
    per_kv = heads_dev // kv_dev
    queries, fresh = gather(
        hidden_in, norm_gain, query_weight, key_weight, value_weight, seq_count
    )
    entries, counts = page_lists(
        cached_lengths, group_ids, prompt_pages, own_pages, key_cache.shape[0], seq_index
    )
    my_start = seq_index * tok_rows
    home = my_start // ADDED_TOKENS
    meta = jnp.stack([home, my_start - home * ADDED_TOKENS]).astype(jnp.int32)
    partial_value, log_scale = attend(
        entries, counts, meta, queries, fresh, key_cache, value_cache, per_kv, tok_rows
    )
    return finish(partial_value, log_scale, out_weight, seq_count, lax.axis_size("tensor"))


def solution(mesh):
    in_specs = (
        P("seq", None),
        P(),
        P(None, "tensor"),
        P(None, "tensor"),
        P(None, "tensor"),
        P("tensor", None),
        P("seq", None, "tensor"),
        P("seq", None, "tensor"),
        P(),
        P(),
        P(),
        P(),
    )
    out_specs = P("seq", "tensor")
    return jax.shard_map(body, mesh=mesh, in_specs=in_specs, out_specs=out_specs, check_vma=False)
```

```python
import functools
import math

import jax
import jax.numpy as jnp
from jax import lax
from jax.experimental import pallas as pl
from jax.experimental.pallas import tpu as pltpu
from jax.sharding import PartitionSpec as P

HEAD_DIM = 128
PAGE_ROWS = 128
ADDED_TOKENS = 512
GROUPS = 2
PROMPT_PAGES = 128
STEP_PAGES = 4
ROW_CHUNK = 256
SCORE_SCALE = 1.0 / math.sqrt(HEAD_DIM)
EXP2_SCALE = SCORE_SCALE * math.log2(math.e)
EMPTY = -1e30
LINES = 8
MESH = pl.DeviceIdType.MESH


def in_hbm(array):
    return pltpu.with_memory_space_constraint(array, pltpu.HBM)


def dot_nt(left, right):
    return lax.dot_general(
        left, right, (((1,), (1,)), ((), ())), preferred_element_type=jnp.float32
    )


def attend_kernel(
    per_kv,
    tok_rows,
    entries,
    counts,
    meta,
    q_ref,
    fresh_ref,
    kc_hbm,
    vc_hbm,
    o_ref,
    ls_ref,
    kc_ref,
    vc_ref,
    m_ref,
    acc_ref,
    load_sem,
):
    loads = [
        pltpu.make_async_copy(kc_hbm, kc_ref, load_sem.at[0]),
        pltpu.make_async_copy(vc_hbm, vc_ref, load_sem.at[1]),
    ]
    for load in loads:
        load.start()
    total_rows = q_ref.shape[0]
    heads = m_ref.shape[0]
    kv_count = heads // per_kv
    ls_ref[...] = jnp.zeros_like(ls_ref)
    m_ref[...] = jnp.full_like(m_ref, EMPTY)
    acc_ref[...] = jnp.zeros_like(acc_ref)

    def cols(index):
        return slice(index * HEAD_DIM, (index + 1) * HEAD_DIM)

    start = pl.multiple_of(meta[0], tok_rows)
    row = lax.broadcasted_iota(jnp.int32, (tok_rows, ADDED_TOKENS), 0)
    col = lax.broadcasted_iota(jnp.int32, (tok_rows, ADDED_TOKENS), 1)
    live = col <= row + meta[1]
    ones = jnp.ones((ADDED_TOKENS, HEAD_DIM), jnp.bfloat16)
    for head in range(heads):
        kv = head // per_kv
        scores = dot_nt(q_ref[pl.ds(start, tok_rows), cols(head)], fresh_ref[:, cols(kv)])
        scores = jnp.where(live, scores, EMPTY)
        top = jnp.max(scores, axis=1, keepdims=True)
        weights = jnp.exp2((scores - top) * EXP2_SCALE).astype(jnp.bfloat16)
        values = jnp.concatenate([fresh_ref[:, cols(kv_count + kv)], ones], axis=1)
        m_ref[head, pl.ds(start, tok_rows), :] = jnp.broadcast_to(top, (tok_rows, HEAD_DIM))
        acc_ref[head, pl.ds(start, tok_rows), :] = jnp.dot(
            weights, values, preferred_element_type=jnp.float32
        )
    for load in loads:
        load.wait()

    def attend_request(request, carry):
        def step(index, carry):
            picked = [entries[request, index * STEP_PAGES + j] for j in range(STEP_PAGES)]
            lane = lax.broadcasted_iota(jnp.int32, (1, PAGE_ROWS), 1)
            bias = jnp.concatenate(
                [jnp.where(lane < (item & 255), 0.0, EMPTY) for item in picked], axis=1
            )
            pages = [item >> 8 for item in picked]
            ones = jnp.ones((STEP_PAGES * PAGE_ROWS, HEAD_DIM), jnp.bfloat16)
            for kv in range(kv_count):
                keys = jnp.concatenate([kc_ref[page, :, cols(kv)] for page in pages], axis=0)
                values = jnp.concatenate([vc_ref[page, :, cols(kv)] for page in pages], axis=0)
                values = jnp.concatenate([values, ones], axis=1)
                for head in range(kv * per_kv, (kv + 1) * per_kv):
                    for chunk in range(ADDED_TOKENS // ROW_CHUNK):
                        first = request * ADDED_TOKENS + chunk * ROW_CHUNK
                        rows = pl.ds(pl.multiple_of(first, ROW_CHUNK), ROW_CHUNK)
                        scores = dot_nt(q_ref[rows, cols(head)], keys) + bias
                        old = m_ref[head, rows, :]
                        new = jnp.maximum(old, jnp.max(scores, axis=1, keepdims=True))
                        weights = jnp.exp2(
                            (scores - jnp.tile(new, (1, STEP_PAGES))) * EXP2_SCALE
                        ).astype(jnp.bfloat16)
                        keep = jnp.exp2((old - new) * EXP2_SCALE)
                        m_ref[head, rows, :] = new
                        acc_ref[head, rows, :] = acc_ref[head, rows, :] * jnp.tile(
                            keep, (1, 2)
                        ) + jnp.dot(weights, values, preferred_element_type=jnp.float32)
            return carry

        return lax.fori_loop(0, (counts[request] + STEP_PAGES - 1) // STEP_PAGES, step, carry)

    lax.fori_loop(0, total_rows // ADDED_TOKENS, attend_request, 0)
    eye = lax.broadcasted_iota(jnp.int32, (128, 128), 0) == lax.broadcasted_iota(
        jnp.int32, (128, 128), 1
    )
    for head in range(heads):
        den = jnp.maximum(acc_ref[head, :, HEAD_DIM:], 1.0)
        o_ref[:, cols(head)] = (acc_ref[head, :, :HEAD_DIM] / den).astype(jnp.bfloat16)
        scale = m_ref[head] * SCORE_SCALE + jnp.log(den)
        for block in range(total_rows // 128):
            part = scale[block * 128 : (block + 1) * 128]
            line = jnp.sum(jnp.where(eye, part, 0.0), axis=0, keepdims=True)
            for piece in range(128 // tok_rows):
                ls_ref[block * (128 // tok_rows) + piece, head : head + 1, :] = line[
                    :, piece * tok_rows : (piece + 1) * tok_rows
                ]


def attend(entries, counts, meta, queries, fresh, key_cache, value_cache, per_kv, tok_rows):
    total_rows, q_cols = queries.shape
    pages, _, kv_cols = key_cache.shape
    heads = q_cols // HEAD_DIM
    vmem = pl.BlockSpec(memory_space=pltpu.VMEM)
    smem = pl.BlockSpec(memory_space=pltpu.SMEM)
    hbm = pl.BlockSpec(memory_space=pltpu.HBM)
    return pl.pallas_call(
        functools.partial(attend_kernel, per_kv, tok_rows),
        out_shape=(
            jax.ShapeDtypeStruct((total_rows, q_cols), jnp.bfloat16),
            jax.ShapeDtypeStruct((total_rows // tok_rows, LINES, tok_rows), jnp.float32),
        ),
        in_specs=[smem, smem, smem, vmem, vmem, hbm, hbm],
        out_specs=(vmem, vmem),
        scratch_shapes=[
            pltpu.VMEM(key_cache.shape, key_cache.dtype),
            pltpu.VMEM(value_cache.shape, value_cache.dtype),
            pltpu.VMEM((heads, total_rows, HEAD_DIM), jnp.float32),
            pltpu.VMEM((heads, total_rows, 2 * HEAD_DIM), jnp.float32),
            pltpu.SemaphoreType.DMA((2,)),
        ],
        compiler_params=pltpu.CompilerParams(vmem_limit_bytes=48 << 20),
        cost_estimate=pl.CostEstimate(
            flops=4 * pages * PAGE_ROWS * ADDED_TOKENS * q_cols,
            bytes_accessed=4 * pages * PAGE_ROWS * kv_cols,
            transcendentals=pages * PAGE_ROWS * ADDED_TOKENS * heads,
        ),
    )(entries, counts, meta, queries, fresh, in_hbm(key_cache), in_hbm(value_cache))


def page_lists(cached_lengths, group_ids, prompt_pages, own_pages, pages_dev, seq_index):
    own_len = cached_lengths - PROMPT_PAGES * PAGE_ROWS
    onehot = (group_ids[:, None] == jnp.arange(GROUPS, dtype=jnp.int32)[None, :]).astype(jnp.int32)
    request_prompt = jnp.sum(onehot[:, :, None] * prompt_pages[None, :, :], axis=1)
    slots = jnp.concatenate([request_prompt, own_pages], axis=1)
    count = slots.shape[1]
    position = jnp.arange(count, dtype=jnp.int32)
    live = jnp.where(
        position[None, :] < PROMPT_PAGES,
        PAGE_ROWS,
        jnp.clip(own_len[:, None] - (position[None, :] - PROMPT_PAGES) * PAGE_ROWS, 0, PAGE_ROWS),
    )
    owned = (slots // pages_dev == seq_index) & (live > 0)
    marks = owned.astype(jnp.int32)
    before = jnp.sum(
        jnp.where(position[None, None, :] < position[None, :, None], marks[:, None, :], 0), axis=2
    )
    packed = (slots - seq_index * pages_dev) * 256 + live
    length = -(-pages_dev // STEP_PAGES) * STEP_PAGES
    places = jnp.arange(length, dtype=jnp.int32)
    entries = jnp.sum(
        jnp.where(
            owned[:, None, :] & (before[:, None, :] == places[None, :, None]),
            packed[:, None, :],
            0,
        ),
        axis=2,
    )
    return entries, jnp.sum(marks, axis=1)


def greet(peers):
    barrier = pltpu.get_barrier_semaphore()
    for peer in peers:
        pl.semaphore_signal(barrier, inc=1, device_id=peer, device_id_type=MESH)
    pl.semaphore_wait(barrier, len(peers))


def remote(source, target, send_sem, recv_sem, peer):
    return pltpu.make_async_remote_copy(
        src_ref=source,
        dst_ref=target,
        send_sem=send_sem,
        recv_sem=recv_sem,
        device_id=peer,
        device_id_type=MESH,
    )


def gather_kernel(
    seq_count,
    x_ref,
    gain_ref,
    wq_ref,
    wk_ref,
    wv_ref,
    q_ref,
    kv_ref,
    q_send,
    q_recv,
    qy_send,
    qy_recv,
    kv_send,
    kv_recv,
    kvy_send,
    kvy_recv,
    wq_buf,
    wk_buf,
    wv_buf,
    x_buf,
    load_sem,
):
    tok_rows = x_ref.shape[0]
    kv_cols = wk_ref.shape[1]
    loads = [
        pltpu.make_async_copy(source, target, load_sem.at[index])
        for index, (source, target) in enumerate(
            ((x_ref, x_buf), (wq_ref, wq_buf), (wk_ref, wk_buf), (wv_ref, wv_buf))
        )
    ]
    for load in loads:
        load.start()
    me = lax.axis_index("seq")
    tensor = lax.axis_index("tensor")
    outer = seq_count // 2
    span = outer * ADDED_TOKENS // q_ref.shape[0]
    place, side = me // 2, me % 2
    base, inside = (place // span) * span, place % span
    twin = (place * 2 + 1 - side, tensor)

    def line_peer(distance):
        return (place + distance) % outer * 2 + side

    def span_peer(distance):
        return (base + (inside + distance) % span) * 2 + side

    def q_rows(owner):
        return pl.ds(pl.multiple_of(owner * tok_rows, tok_rows), tok_rows)

    def kv_rows(owner):
        local = owner - base * 2
        return pl.ds(pl.multiple_of(local * tok_rows, tok_rows), tok_rows)

    greet([twin] + [(line_peer(distance), tensor) for distance in range(1, outer)])

    loads[0].wait()
    floats = x_buf[...].astype(jnp.float32)
    mean = jnp.mean(floats * floats, axis=-1, keepdims=True)
    normed = (floats * lax.rsqrt(mean + 1e-05) * gain_ref[...]).astype(jnp.bfloat16)

    mine = q_rows(me)
    loads[1].wait()
    q_ref[mine, :] = jnp.dot(normed, wq_buf[...], preferred_element_type=jnp.float32).astype(
        jnp.bfloat16
    )
    started = []
    own = q_ref.at[mine, :]
    for distance in range(1, outer):
        peer = (line_peer(distance), tensor)
        copy = remote(own, own, q_send.at[distance], q_recv.at[distance], peer)
        copy.start()
        started.append(copy)
    copy = remote(own, own, qy_send.at[0], qy_recv.at[0], twin)
    copy.start()
    started.append(copy)

    mine = kv_rows(me)
    loads[2].wait()
    loads[3].wait()
    for start, weight in ((0, wk_buf), (kv_cols, wv_buf)):
        kv_ref[mine, start : start + kv_cols] = jnp.dot(
            normed, weight[...], preferred_element_type=jnp.float32
        ).astype(jnp.bfloat16)
    own = kv_ref.at[mine, :]
    for distance in range(1, span):
        peer = (span_peer(distance), tensor)
        copy = remote(own, own, kv_send.at[distance], kv_recv.at[distance], peer)
        copy.start()
        started.append(copy)
    copy = remote(own, own, kvy_send.at[0], kvy_recv.at[0], twin)
    copy.start()
    started.append(copy)

    late = []
    for distance in range(1, outer):
        owner = line_peer(outer - distance)
        block = q_ref.at[q_rows(owner), :]
        remote(block, block, q_send.at[distance], q_recv.at[distance], twin).wait_recv()
        copy = remote(block, block, qy_send.at[distance], qy_recv.at[distance], twin)
        copy.start()
        started.append(copy)
        if distance < span:
            owner = span_peer(span - distance)
            block = kv_ref.at[kv_rows(owner), :]
            remote(block, block, kv_send.at[distance], kv_recv.at[distance], twin).wait_recv()
            copy = remote(block, block, kvy_send.at[distance], kvy_recv.at[distance], twin)
            copy.start()
            started.append(copy)
    for distance in range(outer):
        owner = (place + outer - distance) % outer * 2 + 1 - side
        block = q_ref.at[q_rows(owner), :]
        late.append(remote(block, block, qy_send.at[distance], qy_recv.at[distance], twin))
    for distance in range(span):
        owner = (base + (inside + span - distance) % span) * 2 + 1 - side
        block = kv_ref.at[kv_rows(owner), :]
        late.append(remote(block, block, kvy_send.at[distance], kvy_recv.at[distance], twin))
    for copy in late:
        copy.wait_recv()
    for copy in started:
        copy.wait_send()


def gather(hidden_in, norm_gain, query_weight, key_weight, value_weight, seq_count):
    tok_rows = hidden_in.shape[0]
    q_cols, kv_cols = query_weight.shape[1], key_weight.shape[1]
    slots = pltpu.SemaphoreType.DMA((seq_count // 2,))
    vmem = pl.BlockSpec(memory_space=pltpu.VMEM)
    hbm = pl.BlockSpec(memory_space=pltpu.HBM)
    return pl.pallas_call(
        functools.partial(gather_kernel, seq_count),
        out_shape=(
            jax.ShapeDtypeStruct((tok_rows * seq_count, q_cols), jnp.bfloat16),
            jax.ShapeDtypeStruct((ADDED_TOKENS, 2 * kv_cols), jnp.bfloat16),
        ),
        in_specs=[hbm, vmem, hbm, hbm, hbm],
        out_specs=(vmem, vmem),
        scratch_shapes=[slots] * 8
        + [
            pltpu.VMEM(weight.shape, weight.dtype)
            for weight in (query_weight, key_weight, value_weight, hidden_in)
        ]
        + [pltpu.SemaphoreType.DMA((4,))],
        compiler_params=pltpu.CompilerParams(
            collective_id=0, has_side_effects=True, vmem_limit_bytes=24 << 20
        ),
    )(
        in_hbm(hidden_in),
        norm_gain.reshape(1, -1),
        in_hbm(query_weight),
        in_hbm(key_weight),
        in_hbm(value_weight),
    )


def finish_kernel(
    seq_count,
    tensor_count,
    part_ref,
    ls_ref,
    w_ref,
    out_ref,
    mix_ref,
    mix_got,
    mls_ref,
    side_got,
    sls_ref,
    gls_ref,
    near_ref,
    near_got,
    far_ref,
    far_got,
    side_send,
    side_recv,
    sls_send,
    sls_recv,
    mix_send,
    mix_recv,
    mls_send,
    mls_recv,
    near_send,
    near_recv,
    far_send,
    far_recv,
):
    tok_rows, out_cols = out_ref.shape
    heads = part_ref.shape[1] // HEAD_DIM
    me = lax.axis_index("seq")
    tensor = lax.axis_index("tensor")
    pair, core = tensor // 2, tensor % 2
    pairs = tensor_count // 2
    twin = (me, pair * 2 + 1 - core)
    outer = seq_count // 2
    place, side = me // 2, me % 2
    beside = (place * 2 + 1 - side, tensor)
    order = sorted(range(1, outer), key=lambda distance: -min(distance, outer - distance))

    def far_pair(distance):
        return (pair + distance) % pairs

    def line(distance, which):
        return (place + distance) % outer * 2 + which

    def rows(owner):
        return pl.ds(pl.multiple_of(owner * tok_rows, tok_rows), tok_rows)

    greet(
        [beside]
        + [(line(distance, side), tensor) for distance in range(1, outer)]
        + [twin]
        + [(me, far_pair(distance) * 2 + core) for distance in range(1, pairs)]
    )
    started = []
    scales, sides, mixes, mix_scales = {}, {}, {}, {}
    for distance in order + [0]:
        scales[distance] = remote(
            ls_ref.at[line(distance, 1 - side)],
            sls_ref.at[distance],
            sls_send.at[distance],
            sls_recv.at[distance],
            beside,
        )
        scales[distance].start()
    for distance in order + [0]:
        sides[distance] = remote(
            part_ref.at[rows(line(distance, 1 - side)), :],
            side_got.at[distance],
            side_send.at[distance],
            side_recv.at[distance],
            beside,
        )
        sides[distance].start()
    for distance in order + [0]:
        scales[distance].wait_recv()
    eye = (
        lax.broadcasted_iota(jnp.int32, (tok_rows, tok_rows), 0)
        == lax.broadcasted_iota(jnp.int32, (tok_rows, tok_rows), 1)
    ).astype(jnp.float32)

    def columns(lines):
        return lax.dot_general(
            eye,
            lines.reshape(-1, tok_rows),
            (((1,), (1,)), ((), ())),
            precision=lax.Precision.HIGHEST,
            preferred_element_type=jnp.float32,
        )

    def weighted(block, shares, index):
        return [
            block[:, head * HEAD_DIM : (head + 1) * HEAD_DIM].astype(jnp.float32)
            * shares[:, index * LINES + head : index * LINES + head + 1]
            for head in range(heads)
        ]

    def plus(left, right):
        return [one + other for one, other in zip(left, right)]

    own_lines = jnp.stack([ls_ref[line(distance, side)] for distance in range(outer)])
    side_lines = sls_ref[...]
    top = jnp.maximum(own_lines, side_lines)
    own_scale, side_scale = jnp.exp(own_lines - top), jnp.exp(side_lines - top)
    both = own_scale + side_scale
    mls_ref[...] = top + jnp.log(both)
    for distance in order:
        mix_scales[distance] = remote(
            mls_ref.at[distance],
            gls_ref.at[distance],
            mls_send.at[distance],
            mls_recv.at[distance],
            (line(distance, side), tensor),
        )
        mix_scales[distance].start()
    own_shares, side_shares = columns(own_scale / both), columns(side_scale / both)

    def mixed(distance):
        return plus(
            weighted(part_ref[rows(line(distance, side)), :], own_shares, distance),
            weighted(side_got[distance], side_shares, distance),
        )

    for distance in order:
        sides[distance].wait_recv()
        mix_ref[distance] = jnp.concatenate(mixed(distance), axis=1).astype(jnp.bfloat16)
        mixes[distance] = remote(
            mix_ref.at[distance],
            mix_got.at[distance],
            mix_send.at[distance],
            mix_recv.at[distance],
            (line(distance, side), tensor),
        )
        mixes[distance].start()
    gls_ref[0] = mls_ref[0]
    for distance in order:
        mix_scales[distance].wait_recv()
    lines = gls_ref[...]
    lines = jnp.exp(lines - jnp.max(lines, axis=0, keepdims=True))
    shares = columns(lines / jnp.sum(lines, axis=0, keepdims=True))
    sides[0].wait_recv()
    total = [
        block * shares[:, head : head + 1] for head, block in enumerate(mixed(0))
    ]
    for distance in order:
        mixes[distance].wait_recv()
        total = plus(total, weighted(mix_got[distance], shares, distance))
    for group in (scales, sides, mixes, mix_scales):
        started.extend(group.values())
    attention = jnp.concatenate(total, axis=1).astype(jnp.bfloat16)

    def terms_for(owner):
        start = pl.multiple_of(owner * out_cols, out_cols)
        return jnp.dot(
            attention, w_ref[:, pl.ds(start, out_cols)], preferred_element_type=jnp.float32
        )

    nears = []
    for distance in list(range(1, pairs)) + [0]:
        near_ref[distance] = terms_for(far_pair(distance) * 2 + 1 - core)
        copy = remote(
            near_ref.at[distance],
            near_got.at[distance],
            near_send.at[distance],
            near_recv.at[distance],
            twin,
        )
        copy.start()
        started.append(copy)
        nears.append((distance, copy))
    fars = []
    for distance, copy in nears[:-1]:
        owner = far_pair(distance) * 2 + core
        terms = terms_for(owner)
        copy.wait_recv()
        far_ref[distance] = terms + near_got[distance]
        copy = remote(
            far_ref.at[distance],
            far_got.at[distance],
            far_send.at[distance],
            far_recv.at[distance],
            (me, owner),
        )
        copy.start()
        started.append(copy)
        fars.append(copy)
    result = terms_for(tensor)
    nears[-1][1].wait_recv()
    result = result + near_got[0]
    for distance in range(1, pairs):
        fars[distance - 1].wait_recv()
        result = result + far_got[distance]
    out_ref[...] = result.astype(jnp.bfloat16)
    for copy in started:
        copy.wait_send()


def finish(partial_value, log_scale, out_weight, seq_count, tensor_count):
    tok_rows = partial_value.shape[0] // seq_count
    out_cols = out_weight.shape[1] // tensor_count
    pairs = tensor_count // 2
    vmem = pl.BlockSpec(memory_space=pltpu.VMEM)
    block = pltpu.VMEM((pairs, tok_rows, out_cols), jnp.float32)
    outer = seq_count // 2
    parts = pltpu.VMEM((outer, tok_rows, partial_value.shape[1]), jnp.bfloat16)
    scales = pltpu.VMEM((outer, LINES, tok_rows), jnp.float32)
    line_sems = pltpu.SemaphoreType.DMA((outer,))
    pair_sems = pltpu.SemaphoreType.DMA((pairs,))
    return pl.pallas_call(
        functools.partial(finish_kernel, seq_count, tensor_count),
        out_shape=jax.ShapeDtypeStruct((tok_rows, out_cols), jnp.bfloat16),
        in_specs=[vmem] * 3,
        out_specs=vmem,
        scratch_shapes=[
            parts,
            parts,
            scales,
            parts,
            scales,
            scales,
            block,
            block,
            block,
            block,
        ]
        + [line_sems] * 8
        + [pair_sems] * 4,
        compiler_params=pltpu.CompilerParams(
            collective_id=1, has_side_effects=True, vmem_limit_bytes=24 << 20
        ),
    )(partial_value, log_scale, out_weight)


def body(
    hidden_in,
    norm_gain,
    query_weight,
    key_weight,
    value_weight,
    out_weight,
    key_cache,
    value_cache,
    cached_lengths,
    group_ids,
    prompt_pages,
    own_pages,
):
    tok_rows = hidden_in.shape[0]
    seq_count = lax.axis_size("seq")
    seq_index = lax.axis_index("seq")
    heads_dev = query_weight.shape[1] // HEAD_DIM
    kv_dev = key_weight.shape[1] // HEAD_DIM
    per_kv = heads_dev // kv_dev
    queries, fresh = gather(
        hidden_in, norm_gain, query_weight, key_weight, value_weight, seq_count
    )
    entries, counts = page_lists(
        cached_lengths, group_ids, prompt_pages, own_pages, key_cache.shape[0], seq_index
    )
    my_start = seq_index * tok_rows
    home = my_start // ADDED_TOKENS
    meta = jnp.stack([my_start, my_start - home * ADDED_TOKENS]).astype(jnp.int32)
    partial_value, log_scale = attend(
        entries, counts, meta, queries, fresh, key_cache, value_cache, per_kv, tok_rows
    )
    return finish(partial_value, log_scale, out_weight, seq_count, lax.axis_size("tensor"))


def solution(mesh):
    in_specs = (
        P("seq", None),
        P(),
        P(None, "tensor"),
        P(None, "tensor"),
        P(None, "tensor"),
        P("tensor", None),
        P("seq", None, "tensor"),
        P("seq", None, "tensor"),
        P(),
        P(),
        P(),
        P(),
    )
    out_specs = P("seq", "tensor")
    return jax.shard_map(body, mesh=mesh, in_specs=in_specs, out_specs=out_specs, check_vma=False)
```

```python
import functools
import math

import jax
import jax.numpy as jnp
from jax import lax
from jax.experimental import pallas as pl
from jax.experimental.pallas import tpu as pltpu
from jax.sharding import PartitionSpec as P

HEAD_DIM = 128
PAGE_ROWS = 128
ADDED_TOKENS = 512
GROUPS = 2
PROMPT_PAGES = 128
STEP_PAGES = 4
ROW_CHUNK = 256
SCORE_SCALE = 1.0 / math.sqrt(HEAD_DIM)
EXP2_SCALE = SCORE_SCALE * math.log2(math.e)
EMPTY = -1e30
LINES = 8
MESH = pl.DeviceIdType.MESH


def in_hbm(array):
    return pltpu.with_memory_space_constraint(array, pltpu.HBM)


def dot_nt(left, right):
    return lax.dot_general(
        left, right, (((1,), (1,)), ((), ())), preferred_element_type=jnp.float32
    )


def attend_kernel(
    per_kv,
    tok_rows,
    entries,
    counts,
    meta,
    q_ref,
    fresh_ref,
    kc_hbm,
    vc_hbm,
    o_ref,
    ls_ref,
    kc_ref,
    vc_ref,
    m_ref,
    acc_ref,
    load_sem,
):
    loads = [
        pltpu.make_async_copy(kc_hbm, kc_ref, load_sem.at[0]),
        pltpu.make_async_copy(vc_hbm, vc_ref, load_sem.at[1]),
    ]
    for load in loads:
        load.start()
    total_rows = q_ref.shape[0]
    heads = m_ref.shape[0]
    kv_count = heads // per_kv
    ls_ref[...] = jnp.zeros_like(ls_ref)
    m_ref[...] = jnp.full_like(m_ref, EMPTY)
    acc_ref[...] = jnp.zeros_like(acc_ref)

    def cols(index):
        return slice(index * HEAD_DIM, (index + 1) * HEAD_DIM)

    start = pl.multiple_of(meta[0], tok_rows)
    row = lax.broadcasted_iota(jnp.int32, (tok_rows, ADDED_TOKENS), 0)
    col = lax.broadcasted_iota(jnp.int32, (tok_rows, ADDED_TOKENS), 1)
    live = col <= row + meta[1]
    ones = jnp.ones((ADDED_TOKENS, HEAD_DIM), jnp.bfloat16)
    for head in range(heads):
        kv = head // per_kv
        scores = dot_nt(q_ref[pl.ds(start, tok_rows), cols(head)], fresh_ref[:, cols(kv)])
        scores = jnp.where(live, scores, EMPTY)
        top = jnp.max(scores, axis=1, keepdims=True)
        weights = jnp.exp2((scores - top) * EXP2_SCALE).astype(jnp.bfloat16)
        values = jnp.concatenate([fresh_ref[:, cols(kv_count + kv)], ones], axis=1)
        m_ref[head, pl.ds(start, tok_rows), :] = jnp.broadcast_to(top, (tok_rows, HEAD_DIM))
        acc_ref[head, pl.ds(start, tok_rows), :] = jnp.dot(
            weights, values, preferred_element_type=jnp.float32
        )
    for load in loads:
        load.wait()

    def attend_request(request, carry):
        def step(index, carry):
            picked = [entries[request, index * STEP_PAGES + j] for j in range(STEP_PAGES)]
            lane = lax.broadcasted_iota(jnp.int32, (1, PAGE_ROWS), 1)
            bias = jnp.concatenate(
                [jnp.where(lane < (item & 255), 0.0, EMPTY) for item in picked], axis=1
            )
            pages = [item >> 8 for item in picked]
            ones = jnp.ones((STEP_PAGES * PAGE_ROWS, HEAD_DIM), jnp.bfloat16)
            for kv in range(kv_count):
                keys = jnp.concatenate([kc_ref[page, :, cols(kv)] for page in pages], axis=0)
                values = jnp.concatenate([vc_ref[page, :, cols(kv)] for page in pages], axis=0)
                values = jnp.concatenate([values, ones], axis=1)
                for head in range(kv * per_kv, (kv + 1) * per_kv):
                    for chunk in range(ADDED_TOKENS // ROW_CHUNK):
                        first = request * ADDED_TOKENS + chunk * ROW_CHUNK
                        rows = pl.ds(pl.multiple_of(first, ROW_CHUNK), ROW_CHUNK)
                        scores = dot_nt(q_ref[rows, cols(head)], keys) + bias
                        old = m_ref[head, rows, :]
                        new = jnp.maximum(old, jnp.max(scores, axis=1, keepdims=True))
                        weights = jnp.exp2(
                            (scores - jnp.tile(new, (1, STEP_PAGES))) * EXP2_SCALE
                        ).astype(jnp.bfloat16)
                        keep = jnp.exp2((old - new) * EXP2_SCALE)
                        m_ref[head, rows, :] = new
                        acc_ref[head, rows, :] = acc_ref[head, rows, :] * jnp.tile(
                            keep, (1, 2)
                        ) + jnp.dot(weights, values, preferred_element_type=jnp.float32)
            return carry

        return lax.fori_loop(0, (counts[request] + STEP_PAGES - 1) // STEP_PAGES, step, carry)

    lax.fori_loop(0, total_rows // ADDED_TOKENS, attend_request, 0)
    eye = lax.broadcasted_iota(jnp.int32, (128, 128), 0) == lax.broadcasted_iota(
        jnp.int32, (128, 128), 1
    )
    for head in range(heads):
        den = jnp.maximum(acc_ref[head, :, HEAD_DIM:], 1.0)
        o_ref[:, cols(head)] = (acc_ref[head, :, :HEAD_DIM] / den).astype(jnp.bfloat16)
        scale = m_ref[head] * SCORE_SCALE + jnp.log(den)
        for block in range(total_rows // 128):
            part = scale[block * 128 : (block + 1) * 128]
            line = jnp.sum(jnp.where(eye, part, 0.0), axis=0, keepdims=True)
            for piece in range(128 // tok_rows):
                ls_ref[block * (128 // tok_rows) + piece, head : head + 1, :] = line[
                    :, piece * tok_rows : (piece + 1) * tok_rows
                ]


def attend(entries, counts, meta, queries, fresh, key_cache, value_cache, per_kv, tok_rows):
    total_rows, q_cols = queries.shape
    pages, _, kv_cols = key_cache.shape
    heads = q_cols // HEAD_DIM
    vmem = pl.BlockSpec(memory_space=pltpu.VMEM)
    smem = pl.BlockSpec(memory_space=pltpu.SMEM)
    hbm = pl.BlockSpec(memory_space=pltpu.HBM)
    return pl.pallas_call(
        functools.partial(attend_kernel, per_kv, tok_rows),
        out_shape=(
            jax.ShapeDtypeStruct((total_rows, q_cols), jnp.bfloat16),
            jax.ShapeDtypeStruct((total_rows // tok_rows, LINES, tok_rows), jnp.float32),
        ),
        in_specs=[smem, smem, smem, vmem, vmem, hbm, hbm],
        out_specs=(vmem, vmem),
        scratch_shapes=[
            pltpu.VMEM(key_cache.shape, key_cache.dtype),
            pltpu.VMEM(value_cache.shape, value_cache.dtype),
            pltpu.VMEM((heads, total_rows, HEAD_DIM), jnp.float32),
            pltpu.VMEM((heads, total_rows, 2 * HEAD_DIM), jnp.float32),
            pltpu.SemaphoreType.DMA((2,)),
        ],
        compiler_params=pltpu.CompilerParams(vmem_limit_bytes=48 << 20),
        cost_estimate=pl.CostEstimate(
            flops=4 * pages * PAGE_ROWS * ADDED_TOKENS * q_cols,
            bytes_accessed=4 * pages * PAGE_ROWS * kv_cols,
            transcendentals=pages * PAGE_ROWS * ADDED_TOKENS * heads,
        ),
    )(entries, counts, meta, queries, fresh, in_hbm(key_cache), in_hbm(value_cache))


def page_lists(cached_lengths, group_ids, prompt_pages, own_pages, pages_dev, seq_index):
    own_len = cached_lengths - PROMPT_PAGES * PAGE_ROWS
    onehot = (group_ids[:, None] == jnp.arange(GROUPS, dtype=jnp.int32)[None, :]).astype(jnp.int32)
    request_prompt = jnp.sum(onehot[:, :, None] * prompt_pages[None, :, :], axis=1)
    slots = jnp.concatenate([request_prompt, own_pages], axis=1)
    count = slots.shape[1]
    position = jnp.arange(count, dtype=jnp.int32)
    live = jnp.where(
        position[None, :] < PROMPT_PAGES,
        PAGE_ROWS,
        jnp.clip(own_len[:, None] - (position[None, :] - PROMPT_PAGES) * PAGE_ROWS, 0, PAGE_ROWS),
    )
    owned = (slots // pages_dev == seq_index) & (live > 0)
    marks = owned.astype(jnp.int32)
    before = jnp.sum(
        jnp.where(position[None, None, :] < position[None, :, None], marks[:, None, :], 0), axis=2
    )
    packed = (slots - seq_index * pages_dev) * 256 + live
    length = -(-pages_dev // STEP_PAGES) * STEP_PAGES
    places = jnp.arange(length, dtype=jnp.int32)
    entries = jnp.sum(
        jnp.where(
            owned[:, None, :] & (before[:, None, :] == places[None, :, None]),
            packed[:, None, :],
            0,
        ),
        axis=2,
    )
    return entries, jnp.sum(marks, axis=1)


def greet(peers):
    barrier = pltpu.get_barrier_semaphore()
    for peer in peers:
        pl.semaphore_signal(barrier, inc=1, device_id=peer, device_id_type=MESH)
    pl.semaphore_wait(barrier, len(peers))


def remote(source, target, send_sem, recv_sem, peer):
    return pltpu.make_async_remote_copy(
        src_ref=source,
        dst_ref=target,
        send_sem=send_sem,
        recv_sem=recv_sem,
        device_id=peer,
        device_id_type=MESH,
    )


def gather_kernel(
    seq_count,
    x_ref,
    gain_ref,
    wq_ref,
    wk_ref,
    wv_ref,
    q_ref,
    kv_ref,
    q_send,
    q_recv,
    qy_send,
    qy_recv,
    kv_send,
    kv_recv,
    kvy_send,
    kvy_recv,
    wq_buf,
    wk_buf,
    wv_buf,
    x_buf,
    load_sem,
):
    tok_rows = x_ref.shape[0]
    kv_cols = wk_ref.shape[1]
    loads = [
        pltpu.make_async_copy(source, target, load_sem.at[index])
        for index, (source, target) in enumerate(
            ((x_ref, x_buf), (wq_ref, wq_buf), (wk_ref, wk_buf), (wv_ref, wv_buf))
        )
    ]
    for load in loads:
        load.start()
    me = lax.axis_index("seq")
    tensor = lax.axis_index("tensor")
    outer = seq_count // 2
    span = outer * ADDED_TOKENS // q_ref.shape[0]
    place, side = me // 2, me % 2
    base, inside = (place // span) * span, place % span
    twin = (place * 2 + 1 - side, tensor)

    def line_peer(distance):
        return (place + distance) % outer * 2 + side

    def span_peer(distance):
        return (base + (inside + distance) % span) * 2 + side

    def q_rows(owner):
        return pl.ds(pl.multiple_of(owner * tok_rows, tok_rows), tok_rows)

    def kv_rows(owner):
        local = owner - base * 2
        return pl.ds(pl.multiple_of(local * tok_rows, tok_rows), tok_rows)

    greet([twin] + [(line_peer(distance), tensor) for distance in range(1, outer)])

    loads[0].wait()
    floats = x_buf[...].astype(jnp.float32)
    mean = jnp.mean(floats * floats, axis=-1, keepdims=True)
    normed = (floats * lax.rsqrt(mean + 1e-05) * gain_ref[...]).astype(jnp.bfloat16)

    mine = q_rows(me)
    loads[1].wait()
    q_ref[mine, :] = jnp.dot(normed, wq_buf[...], preferred_element_type=jnp.float32).astype(
        jnp.bfloat16
    )
    started = []
    own = q_ref.at[mine, :]
    copy = remote(own, own, qy_send.at[0], qy_recv.at[0], twin)
    copy.start()
    started.append(copy)
    for distance in range(1, outer):
        peer = (line_peer(distance), tensor)
        copy = remote(own, own, q_send.at[distance], q_recv.at[distance], peer)
        copy.start()
        started.append(copy)

    mine = kv_rows(me)
    loads[2].wait()
    loads[3].wait()
    for start, weight in ((0, wk_buf), (kv_cols, wv_buf)):
        kv_ref[mine, start : start + kv_cols] = jnp.dot(
            normed, weight[...], preferred_element_type=jnp.float32
        ).astype(jnp.bfloat16)
    own = kv_ref.at[mine, :]
    for distance in range(1, span):
        peer = (span_peer(distance), tensor)
        copy = remote(own, own, kv_send.at[distance], kv_recv.at[distance], peer)
        copy.start()
        started.append(copy)
    copy = remote(own, own, kvy_send.at[0], kvy_recv.at[0], twin)
    copy.start()
    started.append(copy)

    late = []
    for distance in range(1, outer):
        owner = line_peer(outer - distance)
        block = q_ref.at[q_rows(owner), :]
        remote(block, block, q_send.at[distance], q_recv.at[distance], twin).wait_recv()
        copy = remote(block, block, qy_send.at[distance], qy_recv.at[distance], twin)
        copy.start()
        started.append(copy)
        if distance < span:
            owner = span_peer(span - distance)
            block = kv_ref.at[kv_rows(owner), :]
            remote(block, block, kv_send.at[distance], kv_recv.at[distance], twin).wait_recv()
            copy = remote(block, block, kvy_send.at[distance], kvy_recv.at[distance], twin)
            copy.start()
            started.append(copy)
    for distance in range(outer):
        owner = (place + outer - distance) % outer * 2 + 1 - side
        block = q_ref.at[q_rows(owner), :]
        late.append(remote(block, block, qy_send.at[distance], qy_recv.at[distance], twin))
    for distance in range(span):
        owner = (base + (inside + span - distance) % span) * 2 + 1 - side
        block = kv_ref.at[kv_rows(owner), :]
        late.append(remote(block, block, kvy_send.at[distance], kvy_recv.at[distance], twin))
    for copy in late:
        copy.wait_recv()
    for copy in started:
        copy.wait_send()


def gather(hidden_in, norm_gain, query_weight, key_weight, value_weight, seq_count):
    tok_rows = hidden_in.shape[0]
    q_cols, kv_cols = query_weight.shape[1], key_weight.shape[1]
    slots = pltpu.SemaphoreType.DMA((seq_count // 2,))
    vmem = pl.BlockSpec(memory_space=pltpu.VMEM)
    hbm = pl.BlockSpec(memory_space=pltpu.HBM)
    return pl.pallas_call(
        functools.partial(gather_kernel, seq_count),
        out_shape=(
            jax.ShapeDtypeStruct((tok_rows * seq_count, q_cols), jnp.bfloat16),
            jax.ShapeDtypeStruct((ADDED_TOKENS, 2 * kv_cols), jnp.bfloat16),
        ),
        in_specs=[hbm, vmem, hbm, hbm, hbm],
        out_specs=(vmem, vmem),
        scratch_shapes=[slots] * 8
        + [
            pltpu.VMEM(weight.shape, weight.dtype)
            for weight in (query_weight, key_weight, value_weight, hidden_in)
        ]
        + [pltpu.SemaphoreType.DMA((4,))],
        compiler_params=pltpu.CompilerParams(
            collective_id=0, has_side_effects=True, vmem_limit_bytes=24 << 20
        ),
    )(
        in_hbm(hidden_in),
        norm_gain.reshape(1, -1),
        in_hbm(query_weight),
        in_hbm(key_weight),
        in_hbm(value_weight),
    )


def finish_kernel(
    seq_count,
    tensor_count,
    part_ref,
    ls_ref,
    w_ref,
    out_ref,
    mix_ref,
    mix_got,
    mls_ref,
    side_got,
    sls_ref,
    gls_ref,
    near_ref,
    near_got,
    far_ref,
    far_got,
    side_send,
    side_recv,
    sls_send,
    sls_recv,
    mix_send,
    mix_recv,
    mls_send,
    mls_recv,
    near_send,
    near_recv,
    far_send,
    far_recv,
):
    tok_rows, out_cols = out_ref.shape
    heads = part_ref.shape[1] // HEAD_DIM
    me = lax.axis_index("seq")
    tensor = lax.axis_index("tensor")
    pair, core = tensor // 2, tensor % 2
    pairs = tensor_count // 2
    twin = (me, pair * 2 + 1 - core)
    outer = seq_count // 2
    place, side = me // 2, me % 2
    beside = (place * 2 + 1 - side, tensor)
    order = sorted(range(1, outer), key=lambda distance: -min(distance, outer - distance))

    def far_pair(distance):
        return (pair + distance) % pairs

    def line(distance, which):
        return (place + distance) % outer * 2 + which

    def rows(owner):
        return pl.ds(pl.multiple_of(owner * tok_rows, tok_rows), tok_rows)

    greet(
        [beside]
        + [(line(distance, side), tensor) for distance in range(1, outer)]
        + [twin]
        + [(me, far_pair(distance) * 2 + core) for distance in range(1, pairs)]
    )
    started = []
    scales, sides, mixes, mix_scales = {}, {}, {}, {}
    for distance in order + [0]:
        scales[distance] = remote(
            ls_ref.at[line(distance, 1 - side)],
            sls_ref.at[distance],
            sls_send.at[distance],
            sls_recv.at[distance],
            beside,
        )
        scales[distance].start()
    for distance in order + [0]:
        sides[distance] = remote(
            part_ref.at[rows(line(distance, 1 - side)), :],
            side_got.at[distance],
            side_send.at[distance],
            side_recv.at[distance],
            beside,
        )
        sides[distance].start()
    for distance in order + [0]:
        scales[distance].wait_recv()
    eye = (
        lax.broadcasted_iota(jnp.int32, (tok_rows, tok_rows), 0)
        == lax.broadcasted_iota(jnp.int32, (tok_rows, tok_rows), 1)
    ).astype(jnp.float32)

    def columns(lines):
        return lax.dot_general(
            eye,
            lines.reshape(-1, tok_rows),
            (((1,), (1,)), ((), ())),
            precision=lax.Precision.HIGHEST,
            preferred_element_type=jnp.float32,
        )

    def weighted(block, shares, index):
        return [
            block[:, head * HEAD_DIM : (head + 1) * HEAD_DIM].astype(jnp.float32)
            * shares[:, index * LINES + head : index * LINES + head + 1]
            for head in range(heads)
        ]

    def plus(left, right):
        return [one + other for one, other in zip(left, right)]

    own_lines = jnp.stack([ls_ref[line(distance, side)] for distance in range(outer)])
    side_lines = sls_ref[...]
    top = jnp.maximum(own_lines, side_lines)
    own_scale, side_scale = jnp.exp(own_lines - top), jnp.exp(side_lines - top)
    both = own_scale + side_scale
    mls_ref[...] = top + jnp.log(both)
    for distance in order:
        mix_scales[distance] = remote(
            mls_ref.at[distance],
            gls_ref.at[distance],
            mls_send.at[distance],
            mls_recv.at[distance],
            (line(distance, side), tensor),
        )
        mix_scales[distance].start()
    own_shares, side_shares = columns(own_scale / both), columns(side_scale / both)

    def mixed(distance):
        return plus(
            weighted(part_ref[rows(line(distance, side)), :], own_shares, distance),
            weighted(side_got[distance], side_shares, distance),
        )

    for distance in order:
        sides[distance].wait_recv()
        mix_ref[distance] = jnp.concatenate(mixed(distance), axis=1).astype(jnp.bfloat16)
        mixes[distance] = remote(
            mix_ref.at[distance],
            mix_got.at[distance],
            mix_send.at[distance],
            mix_recv.at[distance],
            (line(distance, side), tensor),
        )
        mixes[distance].start()
    gls_ref[0] = mls_ref[0]
    for distance in order:
        mix_scales[distance].wait_recv()
    lines = gls_ref[...]
    lines = jnp.exp(lines - jnp.max(lines, axis=0, keepdims=True))
    shares = columns(lines / jnp.sum(lines, axis=0, keepdims=True))
    sides[0].wait_recv()
    total = [
        block * shares[:, head : head + 1] for head, block in enumerate(mixed(0))
    ]
    for distance in order:
        mixes[distance].wait_recv()
        total = plus(total, weighted(mix_got[distance], shares, distance))
    for group in (scales, sides, mixes, mix_scales):
        started.extend(group.values())
    attention = jnp.concatenate(total, axis=1).astype(jnp.bfloat16)

    def terms_for(owner):
        start = pl.multiple_of(owner * out_cols, out_cols)
        return jnp.dot(
            attention, w_ref[:, pl.ds(start, out_cols)], preferred_element_type=jnp.float32
        )

    nears = []
    for distance in list(range(1, pairs)) + [0]:
        near_ref[distance] = terms_for(far_pair(distance) * 2 + 1 - core)
        copy = remote(
            near_ref.at[distance],
            near_got.at[distance],
            near_send.at[distance],
            near_recv.at[distance],
            twin,
        )
        copy.start()
        started.append(copy)
        nears.append((distance, copy))
    fars = []
    for distance, copy in nears[:-1]:
        owner = far_pair(distance) * 2 + core
        terms = terms_for(owner)
        copy.wait_recv()
        far_ref[distance] = terms + near_got[distance]
        copy = remote(
            far_ref.at[distance],
            far_got.at[distance],
            far_send.at[distance],
            far_recv.at[distance],
            (me, owner),
        )
        copy.start()
        started.append(copy)
        fars.append(copy)
    result = terms_for(tensor)
    nears[-1][1].wait_recv()
    result = result + near_got[0]
    for distance in range(1, pairs):
        fars[distance - 1].wait_recv()
        result = result + far_got[distance]
    out_ref[...] = result.astype(jnp.bfloat16)
    for copy in started:
        copy.wait_send()


def finish(partial_value, log_scale, out_weight, seq_count, tensor_count):
    tok_rows = partial_value.shape[0] // seq_count
    out_cols = out_weight.shape[1] // tensor_count
    pairs = tensor_count // 2
    vmem = pl.BlockSpec(memory_space=pltpu.VMEM)
    block = pltpu.VMEM((pairs, tok_rows, out_cols), jnp.float32)
    outer = seq_count // 2
    parts = pltpu.VMEM((outer, tok_rows, partial_value.shape[1]), jnp.bfloat16)
    scales = pltpu.VMEM((outer, LINES, tok_rows), jnp.float32)
    line_sems = pltpu.SemaphoreType.DMA((outer,))
    pair_sems = pltpu.SemaphoreType.DMA((pairs,))
    return pl.pallas_call(
        functools.partial(finish_kernel, seq_count, tensor_count),
        out_shape=jax.ShapeDtypeStruct((tok_rows, out_cols), jnp.bfloat16),
        in_specs=[vmem] * 3,
        out_specs=vmem,
        scratch_shapes=[
            parts,
            parts,
            scales,
            parts,
            scales,
            scales,
            block,
            block,
            block,
            block,
        ]
        + [line_sems] * 8
        + [pair_sems] * 4,
        compiler_params=pltpu.CompilerParams(
            collective_id=1, has_side_effects=True, vmem_limit_bytes=24 << 20
        ),
    )(partial_value, log_scale, out_weight)


def body(
    hidden_in,
    norm_gain,
    query_weight,
    key_weight,
    value_weight,
    out_weight,
    key_cache,
    value_cache,
    cached_lengths,
    group_ids,
    prompt_pages,
    own_pages,
):
    tok_rows = hidden_in.shape[0]
    seq_count = lax.axis_size("seq")
    seq_index = lax.axis_index("seq")
    heads_dev = query_weight.shape[1] // HEAD_DIM
    kv_dev = key_weight.shape[1] // HEAD_DIM
    per_kv = heads_dev // kv_dev
    queries, fresh = gather(
        hidden_in, norm_gain, query_weight, key_weight, value_weight, seq_count
    )
    entries, counts = page_lists(
        cached_lengths, group_ids, prompt_pages, own_pages, key_cache.shape[0], seq_index
    )
    my_start = seq_index * tok_rows
    home = my_start // ADDED_TOKENS
    meta = jnp.stack([my_start, my_start - home * ADDED_TOKENS]).astype(jnp.int32)
    partial_value, log_scale = attend(
        entries, counts, meta, queries, fresh, key_cache, value_cache, per_kv, tok_rows
    )
    return finish(partial_value, log_scale, out_weight, seq_count, lax.axis_size("tensor"))


def solution(mesh):
    in_specs = (
        P("seq", None),
        P(),
        P(None, "tensor"),
        P(None, "tensor"),
        P(None, "tensor"),
        P("tensor", None),
        P("seq", None, "tensor"),
        P("seq", None, "tensor"),
        P(),
        P(),
        P(),
        P(),
    )
    out_specs = P("seq", "tensor")
    return jax.shard_map(body, mesh=mesh, in_specs=in_specs, out_specs=out_specs, check_vma=False)
```
